128 devices in a mesh: grp: 8 (over z, x_lo), lane: 16 (over y, x_hi, core).
Axes of the slice: x: 4 (x_hi: 2, x_lo: 2; x = x_hi * 2 + x_lo), y: 4, z: 4, core: 2. Of those that a mesh axis runs over, the one named last changes fastest.
Arguments:
- factor_left: float32 [4194304], P(('grp', 'lane')), may hold values from -7 to 7, as said below
- denom_right: float32 [4194304], P(('grp', 'lane')), may hold values from -7 to 7, as said below
- bessel_left: float32 [4194304], P(('grp', 'lane')), may hold values from -7 to 7, as said below
- bessel_right: float32 [4194304], P(('grp', 'lane')), may hold values from -7 to 7, as said below
- harmonic_left: float32 [4194304], P(('grp', 'lane')), may hold values from -7 to 7, as said below
- harmonic_right: float32 [4194304], P(('grp', 'lane')), may hold values from -7 to 7, as said below
- weighted_left: float32 [4194304], P(('grp', 'lane')), may hold values from -7 to 7, as said below
Outputs:
- bessel_sum: float32 [8388608], P(('grp', 'lane'))
- harmonic_sum: float32 [8388608], P(('grp', 'lane'))
The draws below stay inside these ranges and needn't reach their ends.
Inputs may be any that keep to these rules, and one draw needn't show every extreme that they name: `factor_left`: every limb is a whole number. `denom_right`: every limb is a whole number. `bessel_left`: every limb is a whole number. `bessel_right`: every limb is a whole number. `harmonic_left`: every limb is a whole number. `harmonic_right`: every limb is a whole number. `weighted_left`: every limb is a whole number.
All inputs are finite; a program needn't handle non-finite values.
Results may differ from the reference program's by a relative error of at most 0.00045.
Values sent between devices are 32-bit elements; how exact they have to be, the bound alone decides.
A program may use at most 128 MiB of HBM per device.

```python
import jax
import jax.numpy as jnp
from jax import lax

LIMB_DEV = 32768
LIMBS = 4194304


def limb_draw(key, salt):
    return jax.random.randint(jax.random.fold_in(key, salt), (LIMBS,), -7, 8).astype(jnp.float32)


def draw_factor_left(key, part):
    return limb_draw(key, 101)


def draw_denom_right(key, part):
    return limb_draw(key, 202)


def draw_bessel_left(key, part):
    return limb_draw(key, 303)


def draw_bessel_right(key, part):
    return limb_draw(key, 404)


def draw_harmonic_left(key, part):
    return limb_draw(key, 505)


def draw_harmonic_right(key, part):
    return limb_draw(key, 606)


def draw_weighted_left(key, part):
    return limb_draw(key, 707)


def setup_inputs(seed: int = 0) -> dict:
    seeds = jax.random.split(jax.random.key(seed), 8)
    factor_left = draw_factor_left(jax.random.fold_in(seeds[7], 71), 0)
    denom_right = draw_denom_right(jax.random.fold_in(seeds[7], 71), 0)
    bessel_left = draw_bessel_left(jax.random.fold_in(seeds[7], 71), 0)
    bessel_right = draw_bessel_right(jax.random.fold_in(seeds[7], 71), 0)
    harmonic_left = draw_harmonic_left(jax.random.fold_in(seeds[7], 71), 0)
    harmonic_right = draw_harmonic_right(jax.random.fold_in(seeds[7], 71), 0)
    weighted_left = draw_weighted_left(jax.random.fold_in(seeds[7], 71), 0)
    return dict(factor_left=factor_left, denom_right=denom_right, bessel_left=bessel_left, bessel_right=bessel_right, harmonic_left=harmonic_left, harmonic_right=harmonic_right, weighted_left=weighted_left)


def combine(earlier, later):
    return (earlier[0] * later[0], earlier[1] * later[0] + later[1])

def carried(values):
    rates = jnp.full(values.shape, jnp.exp(jnp.float32(-1.0 / (2 * LIMB_DEV))), dtype=jnp.float32)
    return lax.associative_scan(combine, (rates, values))[1]

def reference(factor_left, denom_right, bessel_left, bessel_right, harmonic_left, harmonic_right, weighted_left):
    padded = 2 * LIMBS

    def spectrum(limbs):
        return jnp.fft.rfft(limbs, padded)
    factor_spec = spectrum(factor_left)
    denom_spec = spectrum(denom_right)
    bessel_left_spec = spectrum(bessel_left)
    bessel_right_spec = spectrum(bessel_right)
    harmonic_left_spec = spectrum(harmonic_left)
    harmonic_right_spec = spectrum(harmonic_right)
    weighted_spec = spectrum(weighted_left)
    scaling = 1.0 / (16.0 * jnp.sqrt(jnp.float32(LIMBS)) * jnp.sqrt(jnp.float32(LIMB_DEV)))
    bessel = jnp.fft.irfft(bessel_left_spec * denom_spec + factor_spec * bessel_right_spec, padded) * scaling
    harmonic = jnp.fft.irfft(harmonic_left_spec * denom_spec + factor_spec * harmonic_right_spec + weighted_spec * bessel_right_spec, padded) * scaling
    return (carried(bessel.astype(jnp.float32)), carried(harmonic.astype(jnp.float32)))
```

```python
import functools
import math

import jax
import jax.numpy as jnp
import numpy as np
from jax import lax
from jax.experimental import pallas as pl
from jax.experimental.pallas import tpu as pltpu
from jax.sharding import PartitionSpec as P

AXES = ("grp", "lane")
DEVICES = 128
BLOCK = 32768
ROWS = 256
COLS = 128
OPERANDS = 7
OUTPUTS = 2
DECAY = math.exp(-1.0 / (2 * BLOCK))
FIRST = 4 * OPERANDS
SECOND = 16


def split(table):
    high = table.astype(jnp.bfloat16)
    low = (table - high.astype(np.float64)).astype(jnp.bfloat16)
    return high, low


def as_real(table):
    return np.block([[table.real, -table.imag], [table.imag, table.real]])


def unit(turns):
    return np.exp(2j * math.pi * (turns % 1.0))


@functools.lru_cache(maxsize=None)
def tables():
    row = np.arange(ROWS, dtype=np.float64)
    col = np.arange(COLS, dtype=np.float64)
    rows_forward = unit(np.outer(row, row) / ROWS + row[None, :] / (4 * ROWS))
    twist = unit(np.outer(row + 0.25, col) / BLOCK)
    cols_forward = unit(np.outer(col, col) / COLS)
    blocks = np.arange(DEVICES, dtype=np.float64)
    points = np.arange(2 * DEVICES, dtype=np.float64)
    over_blocks = unit(np.outer(points, blocks) / (2 * DEVICES))
    total = DEVICES * BLOCK
    scaling = 1.0 / (16.0 * math.sqrt(total) * math.sqrt(BLOCK)) / (2 * DEVICES) / BLOCK
    order = np.concatenate([2 * blocks, 2 * blocks + 1])
    back_blocks = (
        scaling
        * unit(-np.outer(order, points) / (2 * DEVICES))
        * (1.0 - 1j * unit(points / (2 * DEVICES)))[None, :]
    )
    cols_back = unit(-np.outer(col, col) / COLS)
    rows_back = unit(-(np.outer(row, row) / ROWS + row[:, None] / (4 * ROWS)))
    offset = col[None, :] - col[:, None]
    inside = np.where(offset >= 0, DECAY ** np.maximum(offset, 0), 0.0)
    ends = np.outer(DECAY ** (COLS - 1 - col), DECAY ** (col + 1))
    line = np.arange(2 * ROWS, dtype=np.float64)
    gap = line[:, None] - line[None, :] - 1
    across = np.where(gap >= 0, DECAY ** (COLS * np.maximum(gap, 0)), 0.0)
    forward = (
        *split(np.concatenate([rows_forward.real, rows_forward.imag])),
        twist.real.astype(np.float32),
        twist.imag.astype(np.float32),
        *split(as_real(cols_forward).T),
    )
    middle = (*split(as_real(over_blocks)), *split(as_real(back_blocks)))
    backward = (
        *split(as_real(cols_back).T),
        *split(np.concatenate([rows_back.real, -rows_back.imag], axis=1)),
        *split(np.concatenate([inside, ends], axis=1)),
        *split(across),
    )
    return forward, middle, backward


def halves(values):
    high = values.astype(jnp.bfloat16)
    low = (values - high.astype(jnp.float32)).astype(jnp.bfloat16)
    return high, low


def dot(left, right):
    return jnp.dot(left, right, preferred_element_type=jnp.float32)


def times_table(values, table):
    high, low = halves(values)
    return dot(high, table[0][...]) + dot(high, table[1][...]) + dot(low, table[0][...])


def table_times(table, values):
    high, low = halves(values)
    return dot(table[0][...], high) + dot(table[1][...], high) + dot(table[0][...], low)


def complex_times(left, right):
    return (left[0] * right[0] - left[1] * right[1], left[0] * right[1] + left[1] * right[0])


def forward_kernel(*refs):
    limbs = refs[:OPERANDS]
    rows_high, rows_low, twist_real, twist_imag, cols_high, cols_low, out = refs[OPERANDS:]
    for k in range(OPERANDS):
        whole = limbs[k][...].astype(jnp.bfloat16)
        first = dot(rows_high[...], whole) + dot(rows_low[...], whole)
        turned = complex_times(
            (first[:ROWS], first[ROWS:]), (twist_real[...], twist_imag[...])
        )
        done = times_table(jnp.concatenate(turned, axis=1), (cols_high, cols_low))
        for s in range(2):
            for c in range(2):
                out[pl.ds(4 * k + 2 * s + c, DEVICES, stride=FIRST), :] = done[
                    s * DEVICES : (s + 1) * DEVICES, c * COLS : (c + 1) * COLS
                ]


def middle_kernel(landed, over_high, over_low, back_high, back_low, out):
    def spectrum(k):
        parts = [
            jnp.concatenate(
                [
                    landed[pl.ds(4 * k + 2 * s + c, DEVICES, stride=FIRST), :]
                    for s in range(2)
                ],
                axis=1,
            )
            for c in range(2)
        ]
        both = table_times((over_high, over_low), jnp.concatenate(parts, axis=0))
        return both[: 2 * DEVICES], both[2 * DEVICES :]

    factor, denom, bessel_left, bessel_right, harmonic_left, harmonic_right, weighted = [
        spectrum(k) for k in range(OPERANDS)
    ]

    def added(pairs):
        terms = [complex_times(a, b) for a, b in pairs]
        return sum(t[0] for t in terms), sum(t[1] for t in terms)

    bessel = added([(bessel_left, denom), (factor, bessel_right)])
    harmonic = added(
        [(harmonic_left, denom), (factor, harmonic_right), (weighted, bessel_right)]
    )
    for number, product in enumerate((bessel, harmonic)):
        back = table_times((back_high, back_low), jnp.concatenate(product, axis=0))
        for c in range(2):
            for odd in range(2):
                for s in range(2):
                    start = (2 * c + odd) * DEVICES
                    out[
                        pl.ds(((2 * number + odd) * 2 + s) * 2 + c, DEVICES, stride=SECOND), :
                    ] = back[start : start + DEVICES, s * COLS : (s + 1) * COLS]


def backward_kernel(landed, twist_real, twist_imag, *refs):
    cols_high, cols_low, rows_high, rows_low, scan_high, scan_low, across_high, across_low = refs[:8]
    outs = refs[8:]
    for number in range(OUTPUTS):
        coeffs = []
        for odd in range(2):
            place = (2 * number + odd) * 4
            spectrum = jnp.concatenate(
                [
                    jnp.concatenate(
                        [
                            landed[pl.ds(place + 2 * s + c, DEVICES, stride=SECOND), :]
                            for c in range(2)
                        ],
                        axis=1,
                    )
                    for s in range(2)
                ],
                axis=0,
            )
            first = times_table(spectrum, (cols_high, cols_low))
            turned = complex_times(
                (first[:, :COLS], first[:, COLS:]), (twist_real[...], -twist_imag[...])
            )
            coeffs.append(
                table_times((rows_high, rows_low), jnp.concatenate(turned, axis=0))
            )
        both = times_table(jnp.concatenate(coeffs, axis=0), (scan_high, scan_low))
        outs[number][...] = both[:, :COLS] + table_times(
            (across_high, across_low), both[:, COLS:]
        )


def call(kernel, outs, args):
    return pl.pallas_call(
        kernel,
        out_shape=outs,
        in_specs=[pl.BlockSpec(memory_space=pltpu.VMEM)] * len(args),
        out_specs=jax.tree.map(lambda _: pl.BlockSpec(memory_space=pltpu.VMEM), outs),
        compiler_params=pltpu.CompilerParams(vmem_limit_bytes=48 << 20),
    )(*args)


def exchange(values):
    return lax.all_to_all(values, AXES, split_axis=0, concat_axis=0, tiled=True)


def local(*operands):
    forward, middle, backward = tables()
    limbs = [v.reshape(ROWS, COLS) for v in operands]
    sent = call(
        forward_kernel,
        jax.ShapeDtypeStruct((DEVICES * FIRST, COLS), jnp.float32),
        [*limbs, *forward],
    )
    landed = exchange(sent)
    sent = call(
        middle_kernel,
        jax.ShapeDtypeStruct((DEVICES * SECOND, COLS), jnp.float32),
        [landed, *middle],
    )
    landed = exchange(sent)
    sums = call(
        backward_kernel,
        [jax.ShapeDtypeStruct((2 * ROWS, COLS), jnp.float32)] * OUTPUTS,
        [landed, forward[2], forward[3], *backward],
    )
    sums = jnp.stack([s.reshape(-1) for s in sums])
    everyone = lax.all_gather(sums[:, -1], AXES)
    here = lax.axis_index(AXES)
    gap = here - 1 - lax.iota(jnp.int32, DEVICES)
    weight = jnp.where(gap >= 0, jnp.exp(-jnp.maximum(gap, 0).astype(jnp.float32)), 0.0)
    carry = jnp.sum(everyone * weight[:, None], axis=0)
    power = jnp.exp(-(lax.iota(jnp.float32, 2 * BLOCK) + 1.0) / (2 * BLOCK))
    sums = sums + carry[:, None] * power
    return sums[0], sums[1]


def solution(mesh):
    return jax.shard_map(
        local,
        mesh=mesh,
        in_specs=(P(AXES),) * OPERANDS,
        out_specs=(P(AXES),) * OUTPUTS,
        check_vma=False,
    )
```

```python
import functools
import math

import jax
import jax.numpy as jnp
import numpy as np
from jax import lax
from jax.experimental import pallas as pl
from jax.experimental.pallas import tpu as pltpu
from jax.sharding import PartitionSpec as P

AXES = ("grp", "lane")
DEVICES = 128
BLOCK = 32768
ROWS = 256
COLS = 128
OPERANDS = 7
OUTPUTS = 2
DECAY = math.exp(-1.0 / (2 * BLOCK))
LANES = 16
STEP_IN = 32
STEP_OUT = 16
GROUPS = ((0, 3), (2, 1), (4, 5), (6,))
MESH = pl.DeviceIdType.MESH


def split(table):
    high = table.astype(jnp.bfloat16)
    low = (table - high.astype(np.float64)).astype(jnp.bfloat16)
    return high, low


def as_real(table):
    return np.block([[table.real, -table.imag], [table.imag, table.real]])


def unit(turns):
    return np.exp(2j * math.pi * (turns % 1.0))


@functools.lru_cache(maxsize=None)
def tables():
    row = np.arange(ROWS, dtype=np.float64)
    col = np.arange(COLS, dtype=np.float64)
    rows_forward = unit(np.outer(row, row) / ROWS + row[None, :] / (4 * ROWS))
    twist = unit(np.outer(row + 0.25, col) / BLOCK)
    cols_forward = unit(np.outer(col, col) / COLS)
    blocks = np.arange(DEVICES, dtype=np.float64)
    points = np.arange(2 * DEVICES, dtype=np.float64)
    over_blocks = unit(np.outer(points, blocks) / (2 * DEVICES))
    total = DEVICES * BLOCK
    scaling = 1.0 / (16.0 * math.sqrt(total) * math.sqrt(BLOCK)) / (2 * DEVICES) / BLOCK
    order = np.concatenate([2 * blocks, 2 * blocks + 1])
    back_blocks = (
        scaling
        * unit(-np.outer(order, points) / (2 * DEVICES))
        * (1.0 - 1j * unit(points / (2 * DEVICES)))[None, :]
    )
    cols_back = unit(-np.outer(col, col) / COLS)
    rows_back = unit(-(np.outer(row, row) / ROWS + row[:, None] / (4 * ROWS)))
    offset = col[None, :] - col[:, None]
    inside = np.where(offset >= 0, DECAY ** np.maximum(offset, 0), 0.0)
    ends = np.outer(DECAY ** (COLS - 1 - col), DECAY ** (col + 1))
    line = np.arange(2 * ROWS, dtype=np.float64)
    gap = line[:, None] - line[None, :] - 1
    across = np.where(gap >= 0, DECAY ** (COLS * np.maximum(gap, 0)), 0.0)
    phase = unit((np.arange(ROWS)[:, None] + ROWS * col[None, :] + 0.25) / BLOCK)
    ends_at = DECAY**BLOCK
    reach = (ends_at / DECAY + 1j / DECAY) / (1.0 - 1.0 / (DECAY * phase))
    reach = reach.reshape(2, DEVICES, COLS).transpose(1, 0, 2)
    reach = np.concatenate([reach.real, reach.imag], axis=1)
    reach = np.concatenate([reach, np.zeros_like(reach)], axis=1).astype(np.float32)
    every = np.arange(2 * DEVICES, dtype=np.float64)
    back_all = (
        scaling
        * unit(-np.outer(every, points) / (2 * DEVICES))
        * (1.0 - 1j * unit(points / (2 * DEVICES)))[None, :]
    )
    gap = 2 * blocks[:, None] - 1 - every[None, :]
    carry = np.where(gap >= 0, ends_at ** np.maximum(gap, 0), 0.0) @ back_all
    power = DECAY ** (np.arange(2 * BLOCK, dtype=np.float64) + 1).reshape(2 * ROWS, COLS)
    forward = (
        *split(np.concatenate([rows_forward.real, rows_forward.imag])),
        twist.real.astype(np.float32),
        twist.imag.astype(np.float32),
        *split(as_real(cols_forward).T),
    )
    middle = (
        *split(as_real(over_blocks)),
        *split(as_real(back_blocks)),
        *split(np.concatenate([carry.real, -carry.imag], axis=1)),
    )
    backward = (
        *split(as_real(cols_back).T),
        *split(np.concatenate([rows_back.real, -rows_back.imag], axis=1)),
        *split(np.concatenate([inside, ends], axis=1)),
        *split(across),
    )
    return (*forward, *middle, *backward, power.astype(np.float32), reach)


def halves(values):
    high = values.astype(jnp.bfloat16)
    low = (values - high.astype(jnp.float32)).astype(jnp.bfloat16)
    return high, low


def dot(left, right):
    return jnp.dot(left, right, preferred_element_type=jnp.float32)


def times_table(values, table):
    high, low = halves(values)
    return dot(high, table[0][...]) + dot(high, table[1][...]) + dot(low, table[0][...])


def table_times(table, values):
    high, low = halves(values)
    return dot(table[0][...], high) + dot(table[1][...], high) + dot(table[0][...], low)


def complex_times(left, right):
    return (left[0] * right[0] - left[1] * right[1], left[0] * right[1] + left[1] * right[0])


def block_of(ref, start):
    return ref[pl.ds(start, DEVICES, stride=STEP_IN), :]


def merge_kernel(*refs):
    limbs_in = refs[:OPERANDS]
    count = len(tables())
    tables_in = refs[OPERANDS : OPERANDS + count - 1]
    reach_in = refs[OPERANDS + count - 1]
    outs = refs[OPERANDS + count : OPERANDS + count + OUTPUTS]
    rest = refs[OPERANDS + count + OUTPUTS :]
    limbs = rest[:OPERANDS]
    held = rest[OPERANDS : OPERANDS + count - 1]
    (
        reach,
        sent,
        landed,
        sent_back,
        landed_back,
        results,
        load_sem,
        table_sem,
        out_sem,
        send_sem,
        recv_sem,
        back_send_sem,
        back_recv_sem,
    ) = rest[OPERANDS + count - 1 :]
    (
        rows_high,
        rows_low,
        twist_real,
        twist_imag,
        cols_high,
        cols_low,
        over_high,
        over_low,
        back_high,
        back_low,
        carry_high,
        carry_low,
        cols_back_high,
        cols_back_low,
        rows_back_high,
        rows_back_low,
        scan_high,
        scan_low,
        across_high,
        across_low,
        power,
    ) = held
    me = lax.axis_index("grp") * LANES + lax.axis_index("lane")

    limb_copies = [
        pltpu.make_async_copy(limbs_in[k], limbs[k], load_sem.at[k]) for k in range(OPERANDS)
    ]
    table_copies = [
        pltpu.make_async_copy(tables_in[k], held[k], table_sem.at[k]) for k in range(count - 1)
    ]
    table_copies.append(
        pltpu.make_async_copy(reach_in.at[me], reach, table_sem.at[count - 1])
    )
    loaded = set()

    def need(*numbers):
        for k in numbers:
            if k not in loaded:
                loaded.add(k)
                table_copies[k].wait()

    first_limbs = [k for group in GROUPS for k in group]
    for k in first_limbs[:2]:
        limb_copies[k].start()
    for k in range(6):
        table_copies[k].start()
    for k in first_limbs[2:]:
        limb_copies[k].start()
    for k in range(6, count):
        table_copies[k].start()

    def partner(i):
        other = jnp.bitwise_xor(me, i)
        return other, (lax.div(other, LANES), lax.rem(other, LANES))

    barrier = pltpu.get_barrier_semaphore()

    def greet(i, _):
        pl.semaphore_signal(barrier, inc=1, device_id=partner(i)[1], device_id_type=MESH)
        return 0

    lax.fori_loop(1, DEVICES, greet, 0)

    def send(source, target, step, offset, size, send_to, recv_at):
        def go(i, _):
            other, place = partner(i)
            pltpu.make_async_remote_copy(
                src_ref=source.at[pl.ds(pl.multiple_of(other * step, 8) + offset, size)],
                dst_ref=target.at[pl.ds(pl.multiple_of(me * step, 8) + offset, size)],
                send_sem=send_to,
                recv_sem=recv_at,
                device_id=place,
                device_id_type=MESH,
            ).start()
            return 0

        lax.fori_loop(1, DEVICES, go, 0)
        here = pl.ds(pl.multiple_of(me * step, 8) + offset, size)
        target[here, :] = source[here, :]

    def wait(ref, size, sem):
        whole = ref.at[pl.ds(0, (DEVICES - 1) * size)]
        pltpu.make_async_copy(whole, whole, sem).wait()

    need(0, 1, 2, 3, 4, 5)
    for number, group in enumerate(GROUPS):
        for place, k in enumerate(group):
            limb_copies[k].wait()
            whole = limbs[k][...].astype(jnp.bfloat16)
            first = dot(rows_high[...], whole) + dot(rows_low[...], whole)
            turned = complex_times(
                (first[:ROWS], first[ROWS:]), (twist_real[...], twist_imag[...])
            )
            done = times_table(jnp.concatenate(turned, axis=1), (cols_high, cols_low))
            for s in range(2):
                for c in range(2):
                    start = 8 * number + 4 * place + 2 * s + c
                    sent[pl.ds(start, DEVICES, stride=STEP_IN), :] = done[
                        s * DEVICES : (s + 1) * DEVICES, c * COLS : (c + 1) * COLS
                    ]
        if number == 0:
            pl.semaphore_wait(barrier, DEVICES - 1)
        send(
            sent, landed, STEP_IN, 8 * number, 4 * len(group),
            send_sem.at[number], recv_sem.at[number],
        )

    spectra = [None] * OPERANDS

    def arrive(number):
        group = GROUPS[number]
        wait(landed, 4 * len(group), recv_sem.at[number])
        for place, k in enumerate(group):
            parts = [
                jnp.concatenate(
                    [block_of(landed, 8 * number + 4 * place + 2 * s + c) for s in range(2)],
                    axis=1,
                )
                for c in range(2)
            ]
            both = table_times((over_high, over_low), jnp.concatenate(parts, axis=0))
            spectra[k] = (both[: 2 * DEVICES], both[2 * DEVICES :])

    def give_back(number, terms):
        terms = [complex_times(spectra[a], spectra[b]) for a, b in terms]
        product = (sum(t[0] for t in terms), sum(t[1] for t in terms))
        back = table_times((back_high, back_low), jnp.concatenate(product, axis=0))
        source = sent_back.at[number]
        for c in range(2):
            for odd in range(2):
                for s in range(2):
                    start = (2 * c + odd) * DEVICES
                    source[pl.ds((odd * 2 + s) * 2 + c, DEVICES, stride=STEP_OUT), :] = back[
                        start : start + DEVICES, s * COLS : (s + 1) * COLS
                    ]
        reached = [
            complex_times(
                (product[0][:, s * COLS : (s + 1) * COLS], product[1][:, s * COLS : (s + 1) * COLS]),
                (reach[s : s + 1, :], reach[2 + s : 3 + s, :]),
            )
            for s in range(2)
        ]
        reached = jnp.concatenate(
            [reached[0][0] + reached[1][0], reached[0][1] + reached[1][1]], axis=0
        )
        source[pl.ds(8, DEVICES, stride=STEP_OUT), :] = table_times(
            (carry_high, carry_low), reached
        )
        send(
            source, landed_back.at[number], STEP_OUT, 0, 9,
            back_send_sem.at[number], back_recv_sem.at[number],
        )

    need(6, 7)
    arrive(0)
    arrive(1)
    need(8, 9, 10, 11, count - 1)
    give_back(0, [(2, 1), (0, 3)])
    arrive(2)
    arrive(3)
    give_back(1, [(4, 1), (0, 5), (6, 3)])

    need(*range(count))
    out_copies = []
    for number in range(OUTPUTS):
        source = landed_back.at[number]
        wait(source, 9, back_recv_sem.at[number])
        coeffs = []
        for odd in range(2):
            spectrum = jnp.concatenate(
                [
                    jnp.concatenate(
                        [
                            source[
                                pl.ds(4 * odd + 2 * s + c, DEVICES, stride=STEP_OUT), :
                            ]
                            for c in range(2)
                        ],
                        axis=1,
                    )
                    for s in range(2)
                ],
                axis=0,
            )
            first = times_table(spectrum, (cols_back_high, cols_back_low))
            turned = complex_times(
                (first[:, :COLS], first[:, COLS:]), (twist_real[...], -twist_imag[...])
            )
            coeffs.append(
                table_times((rows_back_high, rows_back_low), jnp.concatenate(turned, axis=0))
            )
        incoming = jnp.sum(source[pl.ds(8, DEVICES, stride=STEP_OUT), :])
        both = times_table(jnp.concatenate(coeffs, axis=0), (scan_high, scan_low))
        results[number] = (
            both[:, :COLS]
            + table_times((across_high, across_low), both[:, COLS:])
            + incoming * power[...]
        )
        copy = pltpu.make_async_copy(results.at[number], outs[number], out_sem.at[number])
        copy.start()
        out_copies.append(copy)

    for copy in out_copies:
        copy.wait()
    for number, group in enumerate(GROUPS):
        wait(sent, 4 * len(group), send_sem.at[number])
    for number in range(OUTPUTS):
        wait(sent_back.at[number], 9, back_send_sem.at[number])


def local(*operands):
    limbs = [v.reshape(ROWS, COLS) for v in operands]
    constants = tables()
    anywhere = pl.BlockSpec(memory_space=pl.ANY)
    sums = pl.pallas_call(
        merge_kernel,
        out_shape=[jax.ShapeDtypeStruct((2 * ROWS, COLS), jnp.float32)] * OUTPUTS,
        in_specs=[anywhere] * (OPERANDS + len(constants)),
        out_specs=[anywhere] * OUTPUTS,
        scratch_shapes=[
            *[pltpu.VMEM((ROWS, COLS), jnp.float32)] * OPERANDS,
            *[pltpu.VMEM(t.shape, t.dtype) for t in constants[:-1]],
            pltpu.VMEM(constants[-1].shape[1:], jnp.float32),
            pltpu.VMEM((DEVICES * STEP_IN, COLS), jnp.float32),
            pltpu.VMEM((DEVICES * STEP_IN, COLS), jnp.float32),
            pltpu.VMEM((OUTPUTS, DEVICES * STEP_OUT, COLS), jnp.float32),
            pltpu.VMEM((OUTPUTS, DEVICES * STEP_OUT, COLS), jnp.float32),
            pltpu.VMEM((OUTPUTS, 2 * ROWS, COLS), jnp.float32),
            pltpu.SemaphoreType.DMA((OPERANDS,)),
            pltpu.SemaphoreType.DMA((len(constants),)),
            pltpu.SemaphoreType.DMA((OUTPUTS,)),
            pltpu.SemaphoreType.DMA((len(GROUPS),)),
            pltpu.SemaphoreType.DMA((len(GROUPS),)),
            pltpu.SemaphoreType.DMA((OUTPUTS,)),
            pltpu.SemaphoreType.DMA((OUTPUTS,)),
        ],
        compiler_params=pltpu.CompilerParams(
            collective_id=0, has_side_effects=True, vmem_limit_bytes=56 << 20
        ),
    )(*limbs, *constants)
    return tuple(s.reshape(-1) for s in sums)


def solution(mesh):
    return jax.shard_map(
        local,
        mesh=mesh,
        in_specs=(P(AXES),) * OPERANDS,
        out_specs=(P(AXES),) * OUTPUTS,
        check_vma=False,
    )
```

```python
import functools
import math

import jax
import jax.numpy as jnp
import numpy as np
from jax import lax
from jax.experimental import pallas as pl
from jax.experimental.pallas import tpu as pltpu
from jax.sharding import PartitionSpec as P

AXES = ("grp", "lane")
DEVICES = 128
BLOCK = 32768
ROWS = 256
COLS = 128
OPERANDS = 7
OUTPUTS = 2
DECAY = math.exp(-1.0 / (2 * BLOCK))
LANES = 16
TEAMS = 8
STEP_IN = 32
STEP_OUT = 8
GROUPS = ((0, 3), (2, 1), (4, 5), (6,))
MESH = pl.DeviceIdType.MESH


def split(table):
    high = table.astype(jnp.bfloat16)
    low = (table - high.astype(np.float64)).astype(jnp.bfloat16)
    return high, low


def as_real(table):
    return np.block([[table.real, -table.imag], [table.imag, table.real]])


def unit(turns):
    return np.exp(2j * math.pi * (turns % 1.0))


@functools.lru_cache(maxsize=None)
def tables():
    row = np.arange(ROWS, dtype=np.float64)
    col = np.arange(COLS, dtype=np.float64)
    rows_forward = unit(np.outer(row, row) / ROWS + row[None, :] / (4 * ROWS))
    twist = unit(np.outer(row + 0.25, col) / BLOCK)
    cols_forward = unit(np.outer(col, col) / COLS)
    blocks = np.arange(DEVICES, dtype=np.float64)
    points = np.arange(2 * DEVICES, dtype=np.float64)
    over_blocks = unit(np.outer(points, blocks) / (2 * DEVICES))
    total = DEVICES * BLOCK
    scaling = 1.0 / (16.0 * math.sqrt(total) * math.sqrt(BLOCK)) / (2 * DEVICES) / BLOCK
    order = np.concatenate([2 * blocks, 2 * blocks + 1])
    back_blocks = (
        scaling
        * unit(-np.outer(order, points) / (2 * DEVICES))
        * (1.0 - 1j * unit(points / (2 * DEVICES)))[None, :]
    )
    cols_back = unit(-np.outer(col, col) / COLS)
    rows_back = unit(-(np.outer(row, row) / ROWS + row[:, None] / (4 * ROWS)))
    offset = col[None, :] - col[:, None]
    inside = np.where(offset >= 0, DECAY ** np.maximum(offset, 0), 0.0)
    ends = np.outer(DECAY ** (COLS - 1 - col), DECAY ** (col + 1))
    line = np.arange(2 * ROWS, dtype=np.float64)
    gap = line[:, None] - line[None, :] - 1
    across = np.where(gap >= 0, DECAY ** (COLS * np.maximum(gap, 0)), 0.0)
    phase = unit((np.arange(ROWS)[:, None] + ROWS * col[None, :] + 0.25) / BLOCK)
    ends_at = DECAY**BLOCK
    reach = (ends_at / DECAY + 1j / DECAY) / (1.0 - 1.0 / (DECAY * phase))
    reach = reach.reshape(2, DEVICES, COLS).transpose(1, 0, 2)
    reach = np.concatenate([reach.real, reach.imag], axis=1)
    reach = np.concatenate([reach, np.zeros_like(reach)], axis=1).astype(np.float32)
    every = np.arange(2 * DEVICES, dtype=np.float64)
    back_all = (
        scaling
        * unit(-np.outer(every, points) / (2 * DEVICES))
        * (1.0 - 1j * unit(points / (2 * DEVICES)))[None, :]
    )
    owner = (blocks.reshape(TEAMS, LANES).T).reshape(-1)
    gap = 2 * owner[:, None] - 1 - every[None, :]
    carry = np.where(gap >= 0, ends_at ** np.maximum(gap, 0), 0.0) @ back_all
    forward = (
        *split(np.concatenate([rows_forward.real, rows_forward.imag])),
        twist.real.astype(np.float32),
        twist.imag.astype(np.float32),
        *split(as_real(cols_forward).T),
    )
    middle = (
        *split(as_real(over_blocks)),
        *split(as_real(back_blocks)),
        *split(np.concatenate([carry.real, -carry.imag], axis=1)),
    )
    backward = (
        *split(as_real(cols_back).T),
        *split(np.concatenate([rows_back.real, -rows_back.imag], axis=1)),
        *split(np.concatenate([inside, ends], axis=1)),
        *split(across),
    )
    return (*forward, *middle, *backward, reach)


def halves(values):
    high = values.astype(jnp.bfloat16)
    low = (values - high.astype(jnp.float32)).astype(jnp.bfloat16)
    return high, low


def dot(left, right):
    return jnp.dot(left, right, preferred_element_type=jnp.float32)


def times_table(values, table):
    high, low = halves(values)
    return dot(high, table[0][...]) + dot(high, table[1][...]) + dot(low, table[0][...])


def table_times(table, values):
    high, low = halves(values)
    return dot(table[0][...], high) + dot(table[1][...], high) + dot(table[0][...], low)


def complex_times(left, right):
    return (left[0] * right[0] - left[1] * right[1], left[0] * right[1] + left[1] * right[0])


def block_of(ref, start):
    return ref[pl.ds(start, DEVICES, stride=STEP_IN), :]


def merge_kernel(*refs):
    limbs_in = refs[:OPERANDS]
    count = len(tables())
    tables_in = refs[OPERANDS : OPERANDS + count - 1]
    reach_in = refs[OPERANDS + count - 1]
    sums_out, carry_out = refs[OPERANDS + count : OPERANDS + count + 2]
    rest = refs[OPERANDS + count + 2 :]
    limbs = rest[:OPERANDS]
    held = rest[OPERANDS : OPERANDS + count - 1]
    (
        reach,
        sent,
        landed,
        sent_back,
        landed_back,
        results,
        owed,
        owed_in,
        part,
        part_in,
        carried,
        load_sem,
        table_sem,
        out_sem,
        send_sem,
        recv_sem,
        back_send_sem,
        back_recv_sem,
        owed_send_sem,
        owed_recv_sem,
        part_send_sem,
        part_recv_sem,
    ) = rest[OPERANDS + count - 1 :]
    (
        rows_high,
        rows_low,
        twist_real,
        twist_imag,
        cols_high,
        cols_low,
        over_high,
        over_low,
        back_high,
        back_low,
        carry_high,
        carry_low,
        cols_back_high,
        cols_back_low,
        rows_back_high,
        rows_back_low,
        scan_high,
        scan_low,
        across_high,
        across_low,
    ) = held
    team, lane = lax.axis_index("grp"), lax.axis_index("lane")
    me = team * LANES + lane

    limb_copies = [
        pltpu.make_async_copy(limbs_in[k], limbs[k], load_sem.at[k]) for k in range(OPERANDS)
    ]
    table_copies = [
        pltpu.make_async_copy(tables_in[k], held[k], table_sem.at[k]) for k in range(count - 1)
    ]
    table_copies.append(
        pltpu.make_async_copy(reach_in.at[me], reach, table_sem.at[count - 1])
    )
    loaded = set()

    def need(*numbers):
        for k in numbers:
            if k not in loaded:
                loaded.add(k)
                table_copies[k].wait()

    first_limbs = [k for group in GROUPS for k in group]
    for k in first_limbs[:2]:
        limb_copies[k].start()
    for k in range(6):
        table_copies[k].start()
    for k in first_limbs[2:]:
        limb_copies[k].start()
    for k in range(6, count):
        table_copies[k].start()

    def partner(i):
        other = jnp.bitwise_xor(me, i)
        return other, (lax.div(other, LANES), lax.rem(other, LANES))

    barrier = pltpu.get_barrier_semaphore()

    def greet(i, _):
        pl.semaphore_signal(barrier, inc=1, device_id=partner(i)[1], device_id_type=MESH)
        return 0

    lax.fori_loop(1, DEVICES, greet, 0)

    def send(source, target, step, offset, size, send_to, recv_at):
        def go(i, _):
            other, place = partner(i)
            pltpu.make_async_remote_copy(
                src_ref=source.at[pl.ds(pl.multiple_of(other * step, 8) + offset, size)],
                dst_ref=target.at[pl.ds(pl.multiple_of(me * step, 8) + offset, size)],
                send_sem=send_to,
                recv_sem=recv_at,
                device_id=place,
                device_id_type=MESH,
            ).start()
            return 0

        lax.fori_loop(1, DEVICES, go, 0)
        here = pl.ds(pl.multiple_of(me * step, 8) + offset, size)
        target[here, :] = source[here, :]

    def wait(ref, size, sem, senders=DEVICES):
        whole = ref.at[pl.ds(0, (senders - 1) * size)]
        pltpu.make_async_copy(whole, whole, sem).wait()

    need(0, 1, 2, 3, 4, 5)
    for number, group in enumerate(GROUPS):
        for place, k in enumerate(group):
            limb_copies[k].wait()
            whole = limbs[k][...].astype(jnp.bfloat16)
            first = dot(rows_high[...], whole) + dot(rows_low[...], whole)
            turned = complex_times(
                (first[:ROWS], first[ROWS:]), (twist_real[...], twist_imag[...])
            )
            done = times_table(jnp.concatenate(turned, axis=1), (cols_high, cols_low))
            for s in range(2):
                for c in range(2):
                    start = 8 * number + 4 * place + 2 * s + c
                    sent[pl.ds(start, DEVICES, stride=STEP_IN), :] = done[
                        s * DEVICES : (s + 1) * DEVICES, c * COLS : (c + 1) * COLS
                    ]
        if number == 0:
            pl.semaphore_wait(barrier, DEVICES - 1)
        send(
            sent, landed, STEP_IN, 8 * number, 4 * len(group),
            send_sem.at[number], recv_sem.at[number],
        )

    spectra = [None] * OPERANDS

    def arrive(number):
        group = GROUPS[number]
        wait(landed, 4 * len(group), recv_sem.at[number])
        for place, k in enumerate(group):
            parts = [
                jnp.concatenate(
                    [block_of(landed, 8 * number + 4 * place + 2 * s + c) for s in range(2)],
                    axis=1,
                )
                for c in range(2)
            ]
            both = table_times((over_high, over_low), jnp.concatenate(parts, axis=0))
            spectra[k] = (both[: 2 * DEVICES], both[2 * DEVICES :])

    def tile(number):
        return pl.ds(pl.multiple_of(number * 8, 8), 8)

    def give_back(number, terms):
        terms = [complex_times(spectra[a], spectra[b]) for a, b in terms]
        product = (sum(t[0] for t in terms), sum(t[1] for t in terms))
        reached = [
            complex_times(
                (product[0][:, s * COLS : (s + 1) * COLS], product[1][:, s * COLS : (s + 1) * COLS]),
                (reach[s : s + 1, :], reach[2 + s : 3 + s, :]),
            )
            for s in range(2)
        ]
        reached = jnp.concatenate(
            [reached[0][0] + reached[1][0], reached[0][1] + reached[1][1]], axis=0
        )
        owed[number] = table_times((carry_high, carry_low), reached)

        def owe(i, _):
            other = jnp.bitwise_xor(lane, i)
            pltpu.make_async_remote_copy(
                src_ref=owed.at[number, tile(other)],
                dst_ref=owed_in.at[number, tile(lane)],
                send_sem=owed_send_sem.at[number],
                recv_sem=owed_recv_sem.at[number],
                device_id=(team, other),
                device_id_type=MESH,
            ).start()
            return 0

        lax.fori_loop(1, LANES, owe, 0)
        owed_in[number, tile(lane), :] = owed[number, tile(lane), :]
        back = table_times((back_high, back_low), jnp.concatenate(product, axis=0))
        source = sent_back.at[number]
        for c in range(2):
            for odd in range(2):
                for s in range(2):
                    start = (2 * c + odd) * DEVICES
                    source[pl.ds((odd * 2 + s) * 2 + c, DEVICES, stride=STEP_OUT), :] = back[
                        start : start + DEVICES, s * COLS : (s + 1) * COLS
                    ]
        send(
            source, landed_back.at[number], STEP_OUT, 0, 8,
            back_send_sem.at[number], back_recv_sem.at[number],
        )

    def gather_owed(number):
        wait(owed_in.at[number], 8, owed_recv_sem.at[number], LANES)
        part[number] = sum(owed_in[number, 8 * k : 8 * k + 8, :] for k in range(LANES))

        def pay(i, _):
            pltpu.make_async_remote_copy(
                src_ref=part.at[number],
                dst_ref=part_in.at[number, tile(team)],
                send_sem=part_send_sem.at[number],
                recv_sem=part_recv_sem.at[number],
                device_id=(jnp.bitwise_xor(team, i), lane),
                device_id_type=MESH,
            ).start()
            return 0

        lax.fori_loop(1, TEAMS, pay, 0)
        part_in[number, tile(team), :] = part[number]

    need(6, 7)
    arrive(0)
    arrive(1)
    need(8, 9, 10, 11, count - 1)
    give_back(0, [(2, 1), (0, 3)])
    arrive(2)
    arrive(3)
    give_back(1, [(4, 1), (0, 5), (6, 3)])

    gather_owed(0)
    gather_owed(1)

    need(*range(count))
    out_copies = []
    for number in range(OUTPUTS):
        source = landed_back.at[number]
        wait(source, 8, back_recv_sem.at[number])
        coeffs = []
        for odd in range(2):
            spectrum = jnp.concatenate(
                [
                    jnp.concatenate(
                        [
                            source[
                                pl.ds(4 * odd + 2 * s + c, DEVICES, stride=STEP_OUT), :
                            ]
                            for c in range(2)
                        ],
                        axis=1,
                    )
                    for s in range(2)
                ],
                axis=0,
            )
            first = times_table(spectrum, (cols_back_high, cols_back_low))
            turned = complex_times(
                (first[:, :COLS], first[:, COLS:]), (twist_real[...], -twist_imag[...])
            )
            coeffs.append(
                table_times((rows_back_high, rows_back_low), jnp.concatenate(turned, axis=0))
            )
        both = times_table(jnp.concatenate(coeffs, axis=0), (scan_high, scan_low))
        results[number] = both[:, :COLS] + table_times(
            (across_high, across_low), both[:, COLS:]
        )
        copy = pltpu.make_async_copy(
            results.at[number], sums_out.at[number], out_sem.at[number]
        )
        copy.start()
        out_copies.append(copy)

    mine = lax.broadcasted_iota(jnp.int32, (8, COLS), 0) == team
    for number in range(OUTPUTS):
        wait(part_in.at[number], 8, part_recv_sem.at[number], TEAMS)
        total = sum(part_in[number, 8 * k : 8 * k + 8, :] for k in range(TEAMS))
        carried[number] = jnp.where(mine, total, 0.0)
    copy = pltpu.make_async_copy(carried, carry_out, out_sem.at[OUTPUTS])
    copy.start()
    out_copies.append(copy)
    for copy in out_copies:
        copy.wait()
    for number, group in enumerate(GROUPS):
        wait(sent, 4 * len(group), send_sem.at[number])
    for number in range(OUTPUTS):
        wait(sent_back.at[number], 8, back_send_sem.at[number])
        wait(owed.at[number], 8, owed_send_sem.at[number], LANES)
        wait(part_in.at[number], 8, part_send_sem.at[number], TEAMS)


def carry_kernel(sums_in, carry_in, *refs):
    outs = refs[:OUTPUTS]
    sums, carry, results, load_sem, out_sem = refs[OUTPUTS:]
    carry_copy = pltpu.make_async_copy(carry_in, carry, load_sem.at[OUTPUTS])
    carry_copy.start()
    copies = [
        pltpu.make_async_copy(sums_in.at[k], sums.at[k], load_sem.at[k]) for k in range(OUTPUTS)
    ]
    for copy in copies:
        copy.start()
    shape = (2 * ROWS, COLS)
    place = lax.broadcasted_iota(jnp.int32, shape, 0) * COLS + lax.broadcasted_iota(
        jnp.int32, shape, 1
    )
    power = jnp.exp((place + 1).astype(jnp.float32) * (-1.0 / (2 * BLOCK)))
    carry_copy.wait()
    out_copies = []
    for k in range(OUTPUTS):
        copies[k].wait()
        results[k] = sums[k] + jnp.sum(carry[k]) * power
        copy = pltpu.make_async_copy(results.at[k], outs[k], out_sem.at[k])
        copy.start()
        out_copies.append(copy)
    for copy in out_copies:
        copy.wait()


def local(*operands):
    limbs = [v.reshape(ROWS, COLS) for v in operands]
    constants = tables()
    anywhere = pl.BlockSpec(memory_space=pl.ANY)
    sums_shape = (OUTPUTS, 2 * ROWS, COLS)
    sums, carry = pl.pallas_call(
        merge_kernel,
        out_shape=[
            jax.ShapeDtypeStruct(sums_shape, jnp.float32),
            jax.ShapeDtypeStruct((OUTPUTS, 8, COLS), jnp.float32),
        ],
        in_specs=[anywhere] * (OPERANDS + len(constants)),
        out_specs=[anywhere] * 2,
        scratch_shapes=[
            *[pltpu.VMEM((ROWS, COLS), jnp.float32)] * OPERANDS,
            *[pltpu.VMEM(t.shape, t.dtype) for t in constants[:-1]],
            pltpu.VMEM(constants[-1].shape[1:], jnp.float32),
            pltpu.VMEM((DEVICES * STEP_IN, COLS), jnp.float32),
            pltpu.VMEM((DEVICES * STEP_IN, COLS), jnp.float32),
            pltpu.VMEM((OUTPUTS, DEVICES * STEP_OUT, COLS), jnp.float32),
            pltpu.VMEM((OUTPUTS, DEVICES * STEP_OUT, COLS), jnp.float32),
            pltpu.VMEM(sums_shape, jnp.float32),
            pltpu.VMEM((OUTPUTS, DEVICES, COLS), jnp.float32),
            pltpu.VMEM((OUTPUTS, DEVICES, COLS), jnp.float32),
            pltpu.VMEM((OUTPUTS, 8, COLS), jnp.float32),
            pltpu.VMEM((OUTPUTS, 8 * TEAMS, COLS), jnp.float32),
            pltpu.VMEM((OUTPUTS, 8, COLS), jnp.float32),
            pltpu.SemaphoreType.DMA((OPERANDS,)),
            pltpu.SemaphoreType.DMA((len(constants),)),
            pltpu.SemaphoreType.DMA((OUTPUTS + 1,)),
            *[pltpu.SemaphoreType.DMA((len(GROUPS),))] * 2,
            *[pltpu.SemaphoreType.DMA((OUTPUTS,))] * 6,
        ],
        compiler_params=pltpu.CompilerParams(
            collective_id=0, has_side_effects=True, vmem_limit_bytes=56 << 20
        ),
    )(*limbs, *constants)
    results = pl.pallas_call(
        carry_kernel,
        out_shape=[jax.ShapeDtypeStruct(sums_shape[1:], jnp.float32)] * OUTPUTS,
        in_specs=[anywhere] * 2,
        out_specs=[anywhere] * OUTPUTS,
        scratch_shapes=[
            pltpu.VMEM(sums_shape, jnp.float32),
            pltpu.VMEM((OUTPUTS, 8, COLS), jnp.float32),
            pltpu.VMEM(sums_shape, jnp.float32),
            pltpu.SemaphoreType.DMA((OUTPUTS + 1,)),
            pltpu.SemaphoreType.DMA((OUTPUTS,)),
        ],
    )(sums, carry)
    return tuple(r.reshape(-1) for r in results)


def solution(mesh):
    return jax.shard_map(
        local,
        mesh=mesh,
        in_specs=(P(AXES),) * OPERANDS,
        out_specs=(P(AXES),) * OUTPUTS,
        check_vma=False,
    )
```

```python
import functools
import math

import jax
import jax.numpy as jnp
import numpy as np
from jax import lax
from jax.experimental import pallas as pl
from jax.experimental.pallas import tpu as pltpu
from jax.sharding import PartitionSpec as P

AXES = ("grp", "lane")
DEVICES = 128
BLOCK = 32768
ROWS = 256
COLS = 128
OPERANDS = 7
OUTPUTS = 2
DECAY = math.exp(-1.0 / (2 * BLOCK))
LANES = 16
TEAMS = 8
STEP_IN = 32
STEP_OUT = 8
GROUPS = ((0, 3), (2, 1), (4, 5), (6,))
MESH = pl.DeviceIdType.MESH


def split(table):
    high = table.astype(jnp.bfloat16)
    low = (table - high.astype(np.float64)).astype(jnp.bfloat16)
    return high, low


def as_real(table):
    return np.block([[table.real, -table.imag], [table.imag, table.real]])


def by_half(table):
    parts = table.reshape(2, 2, DEVICES, -1).transpose(1, 0, 2, 3)
    return parts.reshape(4 * DEVICES, -1)


def unit(turns):
    return np.exp(2j * math.pi * (turns % 1.0))


@functools.lru_cache(maxsize=None)
def tables():
    row = np.arange(ROWS, dtype=np.float64)
    col = np.arange(COLS, dtype=np.float64)
    rows_forward = unit(np.outer(row, row) / ROWS + row[None, :] / (4 * ROWS))
    twist = unit(np.outer(row + 0.25, col) / BLOCK)
    cols_forward = unit(np.outer(col, col) / COLS)
    blocks = np.arange(DEVICES, dtype=np.float64)
    points = np.arange(2 * DEVICES, dtype=np.float64)
    over_blocks = unit(np.outer(points, blocks) / (2 * DEVICES))
    total = DEVICES * BLOCK
    scaling = 1.0 / (16.0 * math.sqrt(total) * math.sqrt(BLOCK)) / (2 * DEVICES) / BLOCK
    order = np.concatenate([2 * blocks, 2 * blocks + 1])
    back_blocks = (
        scaling
        * unit(-np.outer(order, points) / (2 * DEVICES))
        * (1.0 - 1j * unit(points / (2 * DEVICES)))[None, :]
    )
    cols_back = unit(-np.outer(col, col) / COLS)
    rows_back = unit(-(np.outer(row, row) / ROWS + row[:, None] / (4 * ROWS)))
    offset = col[None, :] - col[:, None]
    inside = np.where(offset >= 0, DECAY ** np.maximum(offset, 0), 0.0)
    ends = np.outer(DECAY ** (COLS - 1 - col), DECAY ** (col + 1))
    gap = row[:, None] - row[None, :] - 1
    across = np.where(gap >= 0, DECAY ** (COLS * np.maximum(gap, 0)), 0.0)
    phase = unit((np.arange(ROWS)[:, None] + ROWS * col[None, :] + 0.25) / BLOCK)
    ends_at = DECAY**BLOCK
    reach = (ends_at / DECAY + 1j / DECAY) / (1.0 - 1.0 / (DECAY * phase))
    reach = reach.reshape(2, DEVICES, COLS).transpose(1, 0, 2)
    reach = np.concatenate([reach.real, reach.imag], axis=1)
    reach = np.concatenate([reach, np.zeros_like(reach)], axis=1).astype(np.float32)
    every = np.arange(2 * DEVICES, dtype=np.float64)
    back_all = (
        scaling
        * unit(-np.outer(every, points) / (2 * DEVICES))
        * (1.0 - 1j * unit(points / (2 * DEVICES)))[None, :]
    )
    owner = (blocks.reshape(TEAMS, LANES).T).reshape(-1)
    gap = 2 * owner[:, None] - 1 - every[None, :]
    carry = np.where(gap >= 0, ends_at ** np.maximum(gap, 0), 0.0) @ back_all
    forward = (
        *split(np.concatenate([rows_forward.real, rows_forward.imag])),
        twist.real.astype(np.float32),
        twist.imag.astype(np.float32),
        *split(as_real(cols_forward).T),
    )
    middle = (
        *split(as_real(over_blocks)),
        *split(by_half(as_real(back_blocks))),
        *split(np.concatenate([carry.real, -carry.imag], axis=1)),
    )
    backward = (
        *split(as_real(cols_back).T),
        *split(np.concatenate([rows_back.real, -rows_back.imag], axis=1)),
        *split(np.concatenate([inside, ends], axis=1)),
        *split(across),
    )
    return (*forward, *middle, *backward, reach)


def halves(values):
    high = values.astype(jnp.bfloat16)
    low = (values - high.astype(jnp.float32)).astype(jnp.bfloat16)
    return high, low


def dot(left, right):
    return jnp.dot(left, right, preferred_element_type=jnp.float32)


def times_table(values, table):
    high, low = halves(values)
    return dot(high, table[0][...]) + dot(high, table[1][...]) + dot(low, table[0][...])


def table_times_halves(table, values):
    high, low = values
    return dot(table[0], high) + dot(table[1], high) + dot(table[0], low)


def table_times(table, values):
    return table_times_halves((table[0][...], table[1][...]), halves(values))


def complex_times(left, right):
    return (left[0] * right[0] - left[1] * right[1], left[0] * right[1] + left[1] * right[0])


def block_of(ref, start):
    return ref[pl.ds(start, DEVICES, stride=STEP_IN), :]


def merge_kernel(*refs):
    limbs_in = refs[:OPERANDS]
    count = len(tables())
    tables_in = refs[OPERANDS : OPERANDS + count - 1]
    reach_in = refs[OPERANDS + count - 1]
    sums_out, carry_out = refs[OPERANDS + count : OPERANDS + count + 2]
    rest = refs[OPERANDS + count + 2 :]
    limbs = rest[:OPERANDS]
    held = rest[OPERANDS : OPERANDS + count - 1]
    (
        reach,
        sent,
        landed,
        sent_back,
        landed_back,
        owed,
        owed_in,
        part,
        part_in,
        load_sem,
        table_sem,
        send_sem,
        recv_sem,
        back_send_sem,
        back_recv_sem,
        owed_send_sem,
        owed_recv_sem,
        part_send_sem,
        part_recv_sem,
    ) = rest[OPERANDS + count - 1 :]
    (
        rows_high,
        rows_low,
        twist_real,
        twist_imag,
        cols_high,
        cols_low,
        over_high,
        over_low,
        back_high,
        back_low,
        carry_high,
        carry_low,
        cols_back_high,
        cols_back_low,
        rows_back_high,
        rows_back_low,
        scan_high,
        scan_low,
        across_high,
        across_low,
    ) = held
    team, lane = lax.axis_index("grp"), lax.axis_index("lane")
    me = team * LANES + lane

    limb_copies = [
        pltpu.make_async_copy(limbs_in[k], limbs[k], load_sem.at[k]) for k in range(OPERANDS)
    ]
    table_copies = [
        pltpu.make_async_copy(tables_in[k], held[k], table_sem.at[k]) for k in range(count - 1)
    ]
    table_copies.append(
        pltpu.make_async_copy(reach_in.at[me], reach, table_sem.at[count - 1])
    )
    loaded = set()

    def need(*numbers):
        for k in numbers:
            if k not in loaded:
                loaded.add(k)
                table_copies[k].wait()

    first_limbs = [k for group in GROUPS for k in group]
    for k in first_limbs[:2]:
        limb_copies[k].start()
    for k in range(6):
        table_copies[k].start()

    def partner(i):
        other = jnp.bitwise_xor(me, i)
        return other, (lax.div(other, LANES), lax.rem(other, LANES))

    barrier = pltpu.get_barrier_semaphore()

    def greet(i, _):
        pl.semaphore_signal(barrier, inc=1, device_id=partner(i)[1], device_id_type=MESH)
        return 0

    lax.fori_loop(1, DEVICES, greet, 0)
    for k in first_limbs[2:]:
        limb_copies[k].start()
    for k in range(6, count):
        table_copies[k].start()

    def send(source, target, step, offset, size, send_to, recv_at):
        def go(i, _):
            other, place = partner(i)
            pltpu.make_async_remote_copy(
                src_ref=source.at[pl.ds(pl.multiple_of(other * step, 8) + offset, size)],
                dst_ref=target.at[pl.ds(pl.multiple_of(me * step, 8) + offset, size)],
                send_sem=send_to,
                recv_sem=recv_at,
                device_id=place,
                device_id_type=MESH,
            ).start()
            return 0

        lax.fori_loop(1, DEVICES, go, 0)
        here = pl.ds(pl.multiple_of(me * step, 8) + offset, size)
        target[here, :] = source[here, :]

    def wait(ref, size, sem, senders=DEVICES):
        whole = ref.at[pl.ds(0, (senders - 1) * size)]
        pltpu.make_async_copy(whole, whole, sem).wait()

    def transform(number):
        for place, k in enumerate(GROUPS[number]):
            limb_copies[k].wait()
            whole = limbs[k][...].astype(jnp.bfloat16)
            first = dot(rows_high[...], whole) + dot(rows_low[...], whole)
            turned = complex_times(
                (first[:ROWS], first[ROWS:]), (twist_real[...], twist_imag[...])
            )
            done = times_table(jnp.concatenate(turned, axis=1), (cols_high, cols_low))
            for s in range(2):
                for c in range(2):
                    start = 8 * number + 4 * place + 2 * s + c
                    sent[pl.ds(start, DEVICES, stride=STEP_IN), :] = done[
                        s * DEVICES : (s + 1) * DEVICES, c * COLS : (c + 1) * COLS
                    ]

    def send_group(number):
        send(
            sent, landed, STEP_IN, 8 * number, 4 * len(GROUPS[number]),
            send_sem.at[number], recv_sem.at[number],
        )

    spectra = [None] * OPERANDS
    multiplied = [None] * OUTPUTS

    def arrive(number):
        group = GROUPS[number]
        wait(landed, 4 * len(group), recv_sem.at[number])
        for place, k in enumerate(group):
            parts = [
                jnp.concatenate(
                    [block_of(landed, 8 * number + 4 * place + 2 * s + c) for s in range(2)],
                    axis=1,
                )
                for c in range(2)
            ]
            both = table_times((over_high, over_low), jnp.concatenate(parts, axis=0))
            spectra[k] = (both[: 2 * DEVICES], both[2 * DEVICES :])

    def tile(number):
        return pl.ds(pl.multiple_of(number * 8, 8), 8)

    def multiply(number, terms):
        terms = [complex_times(spectra[a], spectra[b]) for a, b in terms]
        product = (sum(t[0] for t in terms), sum(t[1] for t in terms))
        reached = [
            complex_times(
                (product[0][:, s * COLS : (s + 1) * COLS], product[1][:, s * COLS : (s + 1) * COLS]),
                (reach[s : s + 1, :], reach[2 + s : 3 + s, :]),
            )
            for s in range(2)
        ]
        reached = jnp.concatenate(
            [reached[0][0] + reached[1][0], reached[0][1] + reached[1][1]], axis=0
        )
        owed[number] = table_times((carry_high, carry_low), reached)

        def owe(i, _):
            other = jnp.bitwise_xor(lane, i)
            pltpu.make_async_remote_copy(
                src_ref=owed.at[number, tile(other)],
                dst_ref=owed_in.at[number, tile(lane)],
                send_sem=owed_send_sem.at[number],
                recv_sem=owed_recv_sem.at[number],
                device_id=(team, other),
                device_id_type=MESH,
            ).start()
            return 0

        lax.fori_loop(1, LANES, owe, 0)
        owed_in[number, tile(lane), :] = owed[number, tile(lane), :]
        multiplied[number] = halves(jnp.concatenate(product, axis=0))

    def invert(number, odd):
        rows = slice(2 * odd * DEVICES, 2 * (odd + 1) * DEVICES)
        back = table_times_halves((back_high[rows, :], back_low[rows, :]), multiplied[number])
        source = sent_back.at[number, odd]
        for c in range(2):
            for s in range(2):
                source[pl.ds(2 * s + c, DEVICES, stride=STEP_OUT), :] = back[
                    c * DEVICES : (c + 1) * DEVICES, s * COLS : (s + 1) * COLS
                ]

    def send_back(number, odd):
        send(
            sent_back.at[number, odd], landed_back.at[number, odd], STEP_OUT, 0, 4,
            back_send_sem.at[number, odd], back_recv_sem.at[number, odd],
        )

    def gather_owed(number):
        wait(owed_in.at[number], 8, owed_recv_sem.at[number], LANES)
        part[number] = sum(owed_in[number, 8 * k : 8 * k + 8, :] for k in range(LANES))

        def pay(i, _):
            pltpu.make_async_remote_copy(
                src_ref=part.at[number],
                dst_ref=part_in.at[number, tile(team)],
                send_sem=part_send_sem.at[number],
                recv_sem=part_recv_sem.at[number],
                device_id=(jnp.bitwise_xor(team, i), lane),
                device_id_type=MESH,
            ).start()
            return 0

        lax.fori_loop(1, TEAMS, pay, 0)
        part_in[number, tile(team), :] = part[number]

    def finish(number, odd):
        source = landed_back.at[number, odd]
        wait(source, 4, back_recv_sem.at[number, odd])
        spectrum = jnp.concatenate(
            [
                jnp.concatenate(
                    [source[pl.ds(2 * s + c, DEVICES, stride=STEP_OUT), :] for c in range(2)],
                    axis=1,
                )
                for s in range(2)
            ],
            axis=0,
        )
        first = times_table(spectrum, (cols_back_high, cols_back_low))
        turned = complex_times(
            (first[:, :COLS], first[:, COLS:]), (twist_real[...], -twist_imag[...])
        )
        coeffs = table_times((rows_back_high, rows_back_low), jnp.concatenate(turned, axis=0))
        both = times_table(coeffs, (scan_high, scan_low))
        sums_out[number, odd * ROWS : (odd + 1) * ROWS, :] = both[:, :COLS] + table_times(
            (across_high, across_low), both[:, COLS:]
        )

    need(0, 1, 2, 3, 4, 5)
    transform(0)
    transform(1)
    pl.semaphore_wait(barrier, DEVICES - 1)
    send_group(0)
    send_group(1)
    transform(2)
    transform(3)
    send_group(2)
    send_group(3)
    need(6, 7)
    arrive(0)
    arrive(1)
    need(8, 9, 10, 11, count - 1)
    multiply(0, [(2, 1), (0, 3)])
    invert(0, 0)
    send_back(0, 0)
    invert(0, 1)
    send_back(0, 1)
    arrive(2)
    arrive(3)
    multiply(1, [(4, 1), (0, 5), (6, 3)])
    invert(1, 0)
    send_back(1, 0)
    invert(1, 1)
    send_back(1, 1)
    gather_owed(0)
    gather_owed(1)
    need(*range(count))
    finish(0, 0)
    finish(0, 1)
    finish(1, 0)
    finish(1, 1)

    mine = lax.broadcasted_iota(jnp.int32, (8, COLS), 0) == team
    for number in range(OUTPUTS):
        wait(part_in.at[number], 8, part_recv_sem.at[number], TEAMS)
        total = sum(part_in[number, 8 * k : 8 * k + 8, :] for k in range(TEAMS))
        carry_out[number] = jnp.where(mine, total, 0.0)
    for number, group in enumerate(GROUPS):
        wait(sent, 4 * len(group), send_sem.at[number])
    for number in range(OUTPUTS):
        for odd in range(2):
            wait(sent_back.at[number, odd], 4, back_send_sem.at[number, odd])
        wait(owed.at[number], 8, owed_send_sem.at[number], LANES)
        wait(part_in.at[number], 8, part_send_sem.at[number], TEAMS)


def carry_kernel(sums, carry, *refs):
    outs = refs[:OUTPUTS]
    results, out_sem = refs[OUTPUTS:]
    shape = (ROWS, COLS)
    place = lax.broadcasted_iota(jnp.int32, shape, 0) * COLS + lax.broadcasted_iota(
        jnp.int32, shape, 1
    )
    power = jnp.exp((place + 1).astype(jnp.float32) * (-1.0 / (2 * BLOCK)))
    corner = place[:8, :] == 8 * COLS - 1
    copies = []
    for k in range(OUTPUTS):
        incoming = jnp.sum(carry[k])
        for odd in range(2):
            rows = pl.ds(odd * ROWS, ROWS)
            results[k, rows, :] = sums[k, rows, :] + incoming * power
            copy = pltpu.make_async_copy(
                results.at[k, rows], outs[k].at[rows], out_sem.at[k, odd]
            )
            copy.start()
            copies.append(copy)
            last = sums[k, (odd + 1) * ROWS - 8 : (odd + 1) * ROWS, :]
            incoming = incoming * DECAY**BLOCK + jnp.sum(jnp.where(corner, last, 0.0))
    for copy in copies:
        copy.wait()


def local(*operands):
    limbs = [v.reshape(ROWS, COLS) for v in operands]
    constants = tables()
    anywhere = pl.BlockSpec(memory_space=pl.ANY)
    on_chip = pl.BlockSpec(memory_space=pltpu.VMEM)
    sums_shape = (OUTPUTS, 2 * ROWS, COLS)
    sums, carry = pl.pallas_call(
        merge_kernel,
        out_shape=[
            jax.ShapeDtypeStruct(sums_shape, jnp.float32),
            jax.ShapeDtypeStruct((OUTPUTS, 8, COLS), jnp.float32),
        ],
        in_specs=[anywhere] * (OPERANDS + len(constants)),
        out_specs=[on_chip] * 2,
        scratch_shapes=[
            *[pltpu.VMEM((ROWS, COLS), jnp.float32)] * OPERANDS,
            *[pltpu.VMEM(t.shape, t.dtype) for t in constants[:-1]],
            pltpu.VMEM(constants[-1].shape[1:], jnp.float32),
            pltpu.VMEM((DEVICES * STEP_IN, COLS), jnp.float32),
            pltpu.VMEM((DEVICES * STEP_IN, COLS), jnp.float32),
            *[pltpu.VMEM((OUTPUTS, 2, DEVICES * STEP_OUT, COLS), jnp.float32)] * 2,
            pltpu.VMEM((OUTPUTS, DEVICES, COLS), jnp.float32),
            pltpu.VMEM((OUTPUTS, DEVICES, COLS), jnp.float32),
            pltpu.VMEM((OUTPUTS, 8, COLS), jnp.float32),
            pltpu.VMEM((OUTPUTS, 8 * TEAMS, COLS), jnp.float32),
            pltpu.SemaphoreType.DMA((OPERANDS,)),
            pltpu.SemaphoreType.DMA((len(constants),)),
            *[pltpu.SemaphoreType.DMA((len(GROUPS),))] * 2,
            *[pltpu.SemaphoreType.DMA((OUTPUTS, 2))] * 2,
            *[pltpu.SemaphoreType.DMA((OUTPUTS,))] * 4,
        ],
        compiler_params=pltpu.CompilerParams(
            collective_id=0, has_side_effects=True, vmem_limit_bytes=40 << 20
        ),
    )(*[pltpu.with_memory_space_constraint(v, pltpu.HBM) for v in (*limbs, *constants)])
    results = pl.pallas_call(
        carry_kernel,
        out_shape=[jax.ShapeDtypeStruct(sums_shape[1:], jnp.float32)] * OUTPUTS,
        in_specs=[on_chip] * 2,
        out_specs=[anywhere] * OUTPUTS,
        scratch_shapes=[
            pltpu.VMEM(sums_shape, jnp.float32),
            pltpu.SemaphoreType.DMA((OUTPUTS, 2)),
        ],
        compiler_params=pltpu.CompilerParams(vmem_limit_bytes=8 << 20),
    )(sums, carry)
    return tuple(r.reshape(-1) for r in results)


def solution(mesh):
    return jax.shard_map(
        local,
        mesh=mesh,
        in_specs=(P(AXES),) * OPERANDS,
        out_specs=(P(AXES),) * OUTPUTS,
        check_vma=False,
    )
```

```python
import functools
import math

import jax
import jax.numpy as jnp
import numpy as np
from jax import lax
from jax.experimental import pallas as pl
from jax.experimental.pallas import tpu as pltpu
from jax.sharding import PartitionSpec as P

AXES = ("grp", "lane")
DEVICES = 128
BLOCK = 32768
ROWS = 256
COLS = 128
OPERANDS = 7
OUTPUTS = 2
DECAY = math.exp(-1.0 / (2 * BLOCK))
LANES = 16
TEAMS = 8
RETURN = (8, 4)
STEP_IN = 32
STEP_OUT = 8
GROUPS = ((0, 3), (2, 1), (4, 5), (6,))
MESH = pl.DeviceIdType.MESH


def split(table):
    high = table.astype(jnp.bfloat16)
    low = (table - high.astype(np.float64)).astype(jnp.bfloat16)
    return high, low


def as_real(table):
    return np.block([[table.real, -table.imag], [table.imag, table.real]])


def by_half(table):
    parts = table.reshape(2, 2, DEVICES, -1).transpose(1, 0, 2, 3)
    return parts.reshape(4 * DEVICES, -1)


def unit(turns):
    return np.exp(2j * math.pi * (turns % 1.0))


@functools.lru_cache(maxsize=None)
def tables():
    row = np.arange(ROWS, dtype=np.float64)
    col = np.arange(COLS, dtype=np.float64)
    rows_forward = unit(np.outer(row, row) / ROWS + row[None, :] / (4 * ROWS))
    twist = unit(np.outer(row + 0.25, col) / BLOCK)
    cols_forward = unit(np.outer(col, col) / COLS)
    blocks = np.arange(DEVICES, dtype=np.float64)
    points = np.arange(2 * DEVICES, dtype=np.float64)
    over_blocks = unit(np.outer(points, blocks) / (2 * DEVICES))
    total = DEVICES * BLOCK
    scaling = 1.0 / (16.0 * math.sqrt(total) * math.sqrt(BLOCK)) / (2 * DEVICES) / BLOCK
    order = np.concatenate([2 * blocks, 2 * blocks + 1])
    back_blocks = (
        scaling
        * unit(-np.outer(order, points) / (2 * DEVICES))
        * (1.0 - 1j * unit(points / (2 * DEVICES)))[None, :]
    )
    cols_back = unit(-np.outer(col, col) / COLS)
    rows_back = unit(-(np.outer(row, row) / ROWS + row[:, None] / (4 * ROWS)))
    offset = col[None, :] - col[:, None]
    inside = np.where(offset >= 0, DECAY ** np.maximum(offset, 0), 0.0)
    ends = np.outer(DECAY ** (COLS - 1 - col), DECAY ** (col + 1))
    gap = row[:, None] - row[None, :] - 1
    across = np.where(gap >= 0, DECAY ** (COLS * np.maximum(gap, 0)), 0.0)
    phase = unit((np.arange(ROWS)[:, None] + ROWS * col[None, :] + 0.25) / BLOCK)
    ends_at = DECAY**BLOCK
    reach = (ends_at / DECAY + 1j / DECAY) / (1.0 - 1.0 / (DECAY * phase))
    reach = reach.reshape(2, DEVICES, COLS).transpose(1, 0, 2)
    reach = np.concatenate([reach.real, reach.imag], axis=1)
    reach = np.concatenate([reach, np.zeros_like(reach)], axis=1).astype(np.float32)
    every = np.arange(2 * DEVICES, dtype=np.float64)
    back_all = (
        scaling
        * unit(-np.outer(every, points) / (2 * DEVICES))
        * (1.0 - 1j * unit(points / (2 * DEVICES)))[None, :]
    )
    owner = (blocks.reshape(TEAMS, LANES).T).reshape(-1)
    gap = 2 * owner[:, None] - 1 - every[None, :]
    carry = np.where(gap >= 0, ends_at ** np.maximum(gap, 0), 0.0) @ back_all
    forward = (
        *split(np.concatenate([rows_forward.real, rows_forward.imag])),
        twist.real.astype(np.float32),
        twist.imag.astype(np.float32),
        *split(as_real(cols_forward).T),
    )
    middle = (
        *split(as_real(over_blocks)),
        *split(by_half(as_real(back_blocks))),
        *split(np.concatenate([carry.real, -carry.imag], axis=1)),
    )
    backward = (
        *split(as_real(cols_back).T),
        *split(np.concatenate([rows_back.real, -rows_back.imag], axis=1)),
        *split(np.concatenate([inside, ends], axis=1)),
        *split(across),
    )
    return (*forward, *middle, *backward, reach)


def halves(values):
    high = values.astype(jnp.bfloat16)
    low = (values - high.astype(jnp.float32)).astype(jnp.bfloat16)
    return high, low


def dot(left, right):
    return jnp.dot(left, right, preferred_element_type=jnp.float32)


def times_table(values, table):
    high, low = halves(values)
    return dot(high, table[0][...]) + dot(high, table[1][...]) + dot(low, table[0][...])


def table_times_halves(table, values):
    high, low = values
    return dot(table[0], high) + dot(table[1], high) + dot(table[0], low)


def table_times(table, values):
    return table_times_halves((table[0][...], table[1][...]), halves(values))


def complex_times(left, right):
    return (left[0] * right[0] - left[1] * right[1], left[0] * right[1] + left[1] * right[0])


def block_of(ref, start):
    return ref[pl.ds(start, DEVICES, stride=STEP_IN), :]


def merge_kernel(*refs):
    limbs_in = refs[:OPERANDS]
    count = len(tables())
    tables_in = refs[OPERANDS : OPERANDS + count - 1]
    reach_in = refs[OPERANDS + count - 1]
    sums_out, carry_out = refs[OPERANDS + count : OPERANDS + count + 2]
    rest = refs[OPERANDS + count + 2 :]
    limbs = rest[:OPERANDS]
    held = rest[OPERANDS : OPERANDS + count - 1]
    (
        reach,
        sent,
        landed,
        sent_back,
        landed_back,
        owed,
        owed_in,
        part,
        part_in,
        load_sem,
        table_sem,
        send_sem,
        recv_sem,
        back_send_sem,
        back_recv_sem,
        owed_send_sem,
        owed_recv_sem,
        part_send_sem,
        part_recv_sem,
        relay_sem,
    ) = rest[OPERANDS + count - 1 :]
    (
        rows_high,
        rows_low,
        twist_real,
        twist_imag,
        cols_high,
        cols_low,
        over_high,
        over_low,
        back_high,
        back_low,
        carry_high,
        carry_low,
        cols_back_high,
        cols_back_low,
        rows_back_high,
        rows_back_low,
        scan_high,
        scan_low,
        across_high,
        across_low,
    ) = held
    team, lane = lax.axis_index("grp"), lax.axis_index("lane")
    me = team * LANES + lane

    limb_copies = [
        pltpu.make_async_copy(limbs_in[k], limbs[k], load_sem.at[k]) for k in range(OPERANDS)
    ]
    table_copies = [
        pltpu.make_async_copy(tables_in[k], held[k], table_sem.at[k]) for k in range(count - 1)
    ]
    table_copies.append(
        pltpu.make_async_copy(reach_in.at[me], reach, table_sem.at[count - 1])
    )
    loaded = set()

    def need(*numbers):
        for k in numbers:
            if k not in loaded:
                loaded.add(k)
                table_copies[k].wait()

    first_limbs = [k for group in GROUPS for k in group]
    for k in first_limbs[:2]:
        limb_copies[k].start()
    for k in range(6):
        table_copies[k].start()

    def partner(i):
        other = jnp.bitwise_xor(me, lax.rem(i * 37, DEVICES))
        return other, (lax.div(other, LANES), lax.rem(other, LANES))

    barrier = pltpu.get_barrier_semaphore()

    def greet_lane(i, _):
        other = jnp.bitwise_xor(lane, i)
        pl.semaphore_signal(barrier, inc=1, device_id=(team, other), device_id_type=MESH)
        return 0

    def greet_team(i, _):
        other = jnp.bitwise_xor(team, i)
        pl.semaphore_signal(barrier, inc=1, device_id=(other, lane), device_id_type=MESH)
        return 0

    def relay(i, _):
        other = jnp.bitwise_xor(team, i)
        pl.semaphore_signal(relay_sem, inc=1, device_id=(other, lane), device_id_type=MESH)
        return 0

    lax.fori_loop(1, LANES, greet_lane, 0)
    lax.fori_loop(1, TEAMS, greet_team, 0)
    for k in first_limbs[2:]:
        limb_copies[k].start()
    for k in range(6, count):
        table_copies[k].start()

    def send(source, target, step, offset, size, send_to, recv_at):
        def go(i, _):
            other, place = partner(i)
            pltpu.make_async_remote_copy(
                src_ref=source.at[pl.ds(pl.multiple_of(other * step, 8) + offset, size)],
                dst_ref=target.at[pl.ds(pl.multiple_of(me * step, 8) + offset, size)],
                send_sem=send_to,
                recv_sem=recv_at,
                device_id=place,
                device_id_type=MESH,
            ).start()
            return 0

        lax.fori_loop(1, DEVICES, go, 0)
        here = pl.ds(pl.multiple_of(me * step, 8) + offset, size)
        target[here, :] = source[here, :]

    def wait(ref, size, sem, senders=DEVICES):
        whole = ref.at[pl.ds(0, (senders - 1) * size)]
        pltpu.make_async_copy(whole, whole, sem).wait()

    def transform(number):
        for place, k in enumerate(GROUPS[number]):
            limb_copies[k].wait()
            whole = limbs[k][...].astype(jnp.bfloat16)
            first = dot(rows_high[...], whole) + dot(rows_low[...], whole)
            turned = complex_times(
                (first[:ROWS], first[ROWS:]), (twist_real[...], twist_imag[...])
            )
            done = times_table(jnp.concatenate(turned, axis=1), (cols_high, cols_low))
            for s in range(2):
                for c in range(2):
                    start = 8 * number + 4 * place + 2 * s + c
                    sent[pl.ds(start, DEVICES, stride=STEP_IN), :] = done[
                        s * DEVICES : (s + 1) * DEVICES, c * COLS : (c + 1) * COLS
                    ]

    def send_group(number):
        send(
            sent, landed, STEP_IN, 8 * number, 4 * len(GROUPS[number]),
            send_sem.at[number], recv_sem.at[number],
        )

    spectra = [None] * OPERANDS
    multiplied = [None] * OUTPUTS

    def arrive(number):
        group = GROUPS[number]
        wait(landed, 4 * len(group), recv_sem.at[number])
        for place, k in enumerate(group):
            parts = [
                jnp.concatenate(
                    [block_of(landed, 8 * number + 4 * place + 2 * s + c) for s in range(2)],
                    axis=1,
                )
                for c in range(2)
            ]
            both = table_times((over_high, over_low), jnp.concatenate(parts, axis=0))
            spectra[k] = (both[: 2 * DEVICES], both[2 * DEVICES :])

    def tile(number):
        return pl.ds(pl.multiple_of(number * 8, 8), 8)

    def multiply(number, terms):
        terms = [complex_times(spectra[a], spectra[b]) for a, b in terms]
        product = (sum(t[0] for t in terms), sum(t[1] for t in terms))
        reached = [
            complex_times(
                (product[0][:, s * COLS : (s + 1) * COLS], product[1][:, s * COLS : (s + 1) * COLS]),
                (reach[s : s + 1, :], reach[2 + s : 3 + s, :]),
            )
            for s in range(2)
        ]
        reached = jnp.concatenate(
            [reached[0][0] + reached[1][0], reached[0][1] + reached[1][1]], axis=0
        )
        owed[number] = table_times((carry_high, carry_low), reached)

        def owe(i, _):
            other = jnp.bitwise_xor(lane, i)
            pltpu.make_async_remote_copy(
                src_ref=owed.at[number, tile(other)],
                dst_ref=owed_in.at[number, tile(lane)],
                send_sem=owed_send_sem.at[number],
                recv_sem=owed_recv_sem.at[number],
                device_id=(team, other),
                device_id_type=MESH,
            ).start()
            return 0

        lax.fori_loop(1, LANES, owe, 0)
        owed_in[number, tile(lane), :] = owed[number, tile(lane), :]
        multiplied[number] = halves(jnp.concatenate(product, axis=0))

    def invert(number, odd):
        rows = slice(2 * odd * DEVICES, 2 * (odd + 1) * DEVICES)
        back = table_times_halves((back_high[rows, :], back_low[rows, :]), multiplied[number])
        source = sent_back.at[number, number * odd]
        shift = (1 - number) * 4 * odd
        for c in range(2):
            for s in range(2):
                source[pl.ds(shift + 2 * s + c, DEVICES, stride=STEP_OUT), :] = back[
                    c * DEVICES : (c + 1) * DEVICES, s * COLS : (s + 1) * COLS
                ]

    def send_back(number, odd):
        send(
            sent_back.at[number, odd], landed_back.at[number, odd], STEP_OUT, 0, RETURN[number],
            back_send_sem.at[number, odd], back_recv_sem.at[number, odd],
        )

    def gather_owed(number):
        wait(owed_in.at[number], 8, owed_recv_sem.at[number], LANES)
        part[number] = sum(owed_in[number, 8 * k : 8 * k + 8, :] for k in range(LANES))

        def pay(i, _):
            pltpu.make_async_remote_copy(
                src_ref=part.at[number],
                dst_ref=part_in.at[number, tile(team)],
                send_sem=part_send_sem.at[number],
                recv_sem=part_recv_sem.at[number],
                device_id=(jnp.bitwise_xor(team, i), lane),
                device_id_type=MESH,
            ).start()
            return 0

        lax.fori_loop(1, TEAMS, pay, 0)
        part_in[number, tile(team), :] = part[number]

    def finish(number, odd):
        source = landed_back.at[number, number * odd]
        shift = (1 - number) * 4 * odd
        if number or not odd:
            wait(source, RETURN[number], back_recv_sem.at[number, odd])
        spectrum = jnp.concatenate(
            [
                jnp.concatenate(
                    [
                        source[pl.ds(shift + 2 * s + c, DEVICES, stride=STEP_OUT), :]
                        for c in range(2)
                    ],
                    axis=1,
                )
                for s in range(2)
            ],
            axis=0,
        )
        first = times_table(spectrum, (cols_back_high, cols_back_low))
        turned = complex_times(
            (first[:, :COLS], first[:, COLS:]), (twist_real[...], -twist_imag[...])
        )
        coeffs = table_times((rows_back_high, rows_back_low), jnp.concatenate(turned, axis=0))
        both = times_table(coeffs, (scan_high, scan_low))
        sums_out[number, odd * ROWS : (odd + 1) * ROWS, :] = both[:, :COLS] + table_times(
            (across_high, across_low), both[:, COLS:]
        )

    need(0, 1, 2, 3, 4, 5)
    transform(0)
    pl.semaphore_wait(barrier, LANES + TEAMS - 2)
    lax.fori_loop(1, TEAMS, relay, 0)
    transform(1)
    pl.semaphore_wait(relay_sem, TEAMS - 1)
    send_group(0)
    send_group(1)
    transform(2)
    transform(3)
    send_group(2)
    send_group(3)
    need(6, 7)
    arrive(0)
    arrive(1)
    need(8, 9, 10, 11, count - 1)
    multiply(0, [(2, 1), (0, 3)])
    invert(0, 0)
    invert(0, 1)
    send_back(0, 0)
    arrive(2)
    arrive(3)
    multiply(1, [(4, 1), (0, 5), (6, 3)])
    invert(1, 0)
    send_back(1, 0)
    invert(1, 1)
    send_back(1, 1)
    gather_owed(0)
    gather_owed(1)
    need(*range(count))
    finish(0, 0)
    finish(0, 1)
    finish(1, 0)
    finish(1, 1)

    mine = lax.broadcasted_iota(jnp.int32, (8, COLS), 0) == team
    for number in range(OUTPUTS):
        wait(part_in.at[number], 8, part_recv_sem.at[number], TEAMS)
        total = sum(part_in[number, 8 * k : 8 * k + 8, :] for k in range(TEAMS))
        carry_out[number] = jnp.where(mine, total, 0.0)
    for number, group in enumerate(GROUPS):
        wait(sent, 4 * len(group), send_sem.at[number])
    for number in range(OUTPUTS):
        for odd in range(1 + number):
            wait(
                sent_back.at[number, odd], RETURN[number], back_send_sem.at[number, odd]
            )
        wait(owed.at[number], 8, owed_send_sem.at[number], LANES)
        wait(part_in.at[number], 8, part_send_sem.at[number], TEAMS)


def carry_kernel(sums, carry, *refs):
    outs = refs[:OUTPUTS]
    results, out_sem = refs[OUTPUTS:]
    shape = (ROWS, COLS)
    place = lax.broadcasted_iota(jnp.int32, shape, 0) * COLS + lax.broadcasted_iota(
        jnp.int32, shape, 1
    )
    power = jnp.exp((place + 1).astype(jnp.float32) * (-1.0 / (2 * BLOCK)))
    corner = place[:8, :] == 8 * COLS - 1
    copies = []
    for k in range(OUTPUTS):
        incoming = jnp.sum(carry[k])
        for odd in range(2):
            rows = pl.ds(odd * ROWS, ROWS)
            results[k, rows, :] = sums[k, rows, :] + incoming * power
            copy = pltpu.make_async_copy(
                results.at[k, rows], outs[k].at[rows], out_sem.at[k, odd]
            )
            copy.start()
            copies.append(copy)
            last = sums[k, (odd + 1) * ROWS - 8 : (odd + 1) * ROWS, :]
            incoming = incoming * DECAY**BLOCK + jnp.sum(jnp.where(corner, last, 0.0))
    for copy in copies:
        copy.wait()


def local(*operands):
    limbs = [v.reshape(ROWS, COLS) for v in operands]
    constants = tables()
    anywhere = pl.BlockSpec(memory_space=pl.ANY)
    on_chip = pl.BlockSpec(memory_space=pltpu.VMEM)
    sums_shape = (OUTPUTS, 2 * ROWS, COLS)
    sums, carry = pl.pallas_call(
        merge_kernel,
        out_shape=[
            jax.ShapeDtypeStruct(sums_shape, jnp.float32),
            jax.ShapeDtypeStruct((OUTPUTS, 8, COLS), jnp.float32),
        ],
        in_specs=[anywhere] * (OPERANDS + len(constants)),
        out_specs=[on_chip] * 2,
        scratch_shapes=[
            *[pltpu.VMEM((ROWS, COLS), jnp.float32)] * OPERANDS,
            *[pltpu.VMEM(t.shape, t.dtype) for t in constants[:-1]],
            pltpu.VMEM(constants[-1].shape[1:], jnp.float32),
            pltpu.VMEM((DEVICES * STEP_IN, COLS), jnp.float32),
            pltpu.VMEM((DEVICES * STEP_IN, COLS), jnp.float32),
            *[pltpu.VMEM((OUTPUTS, 2, DEVICES * STEP_OUT, COLS), jnp.float32)] * 2,
            pltpu.VMEM((OUTPUTS, DEVICES, COLS), jnp.float32),
            pltpu.VMEM((OUTPUTS, DEVICES, COLS), jnp.float32),
            pltpu.VMEM((OUTPUTS, 8, COLS), jnp.float32),
            pltpu.VMEM((OUTPUTS, 8 * TEAMS, COLS), jnp.float32),
            pltpu.SemaphoreType.DMA((OPERANDS,)),
            pltpu.SemaphoreType.DMA((len(constants),)),
            *[pltpu.SemaphoreType.DMA((len(GROUPS),))] * 2,
            *[pltpu.SemaphoreType.DMA((OUTPUTS, 2))] * 2,
            *[pltpu.SemaphoreType.DMA((OUTPUTS,))] * 4,
            pltpu.SemaphoreType.REGULAR,
        ],
        compiler_params=pltpu.CompilerParams(
            collective_id=0, has_side_effects=True, vmem_limit_bytes=40 << 20
        ),
    )(*[pltpu.with_memory_space_constraint(v, pltpu.HBM) for v in (*limbs, *constants)])
    results = pl.pallas_call(
        carry_kernel,
        out_shape=[jax.ShapeDtypeStruct(sums_shape[1:], jnp.float32)] * OUTPUTS,
        in_specs=[on_chip] * 2,
        out_specs=[anywhere] * OUTPUTS,
        scratch_shapes=[
            pltpu.VMEM(sums_shape, jnp.float32),
            pltpu.SemaphoreType.DMA((OUTPUTS, 2)),
        ],
        compiler_params=pltpu.CompilerParams(vmem_limit_bytes=8 << 20),
    )(sums, carry)
    return tuple(r.reshape(-1) for r in results)


def solution(mesh):
    return jax.shard_map(
        local,
        mesh=mesh,
        in_specs=(P(AXES),) * OPERANDS,
        out_specs=(P(AXES),) * OUTPUTS,
        check_vma=False,
    )
```

```python
import functools
import math

import jax
import jax.numpy as jnp
import numpy as np
from jax import lax
from jax.experimental import pallas as pl
from jax.experimental.pallas import tpu as pltpu
from jax.sharding import PartitionSpec as P

AXES = ("grp", "lane")
DEVICES = 128
BLOCK = 32768
ROWS = 256
COLS = 128
OPERANDS = 7
OUTPUTS = 2
DECAY = math.exp(-1.0 / (2 * BLOCK))
LANES = 16
TEAMS = 8
STEP_IN = 32
STEP_OUT = 8
GROUPS = ((0, 3), (2, 1), (4, 5), (6,))
SIZES = (8, 8, 6, 6)
MESH = pl.DeviceIdType.MESH


def split(table):
    high = table.astype(jnp.bfloat16)
    low = (table - high.astype(np.float64)).astype(jnp.bfloat16)
    return high, low


def as_real(table):
    return np.block([[table.real, -table.imag], [table.imag, table.real]])


def by_half(table):
    parts = table.reshape(2, 2, DEVICES, -1).transpose(1, 0, 2, 3)
    return parts.reshape(4 * DEVICES, -1)


def unit(turns):
    return np.exp(2j * math.pi * (turns % 1.0))


@functools.lru_cache(maxsize=None)
def tables():
    row = np.arange(ROWS, dtype=np.float64)
    col = np.arange(COLS, dtype=np.float64)
    rows_forward = unit(np.outer(row, row) / ROWS + row[None, :] / (4 * ROWS))
    twist = unit(np.outer(row + 0.25, col) / BLOCK)
    cols_forward = unit(np.outer(col, col) / COLS)
    blocks = np.arange(DEVICES, dtype=np.float64)
    points = np.arange(2 * DEVICES, dtype=np.float64)
    over_blocks = unit(np.outer(points, blocks) / (2 * DEVICES))
    total = DEVICES * BLOCK
    scaling = 1.0 / (16.0 * math.sqrt(total) * math.sqrt(BLOCK)) / (2 * DEVICES) / BLOCK
    order = np.concatenate([2 * blocks, 2 * blocks + 1])
    back_blocks = (
        scaling
        * unit(-np.outer(order, points) / (2 * DEVICES))
        * (1.0 - 1j * unit(points / (2 * DEVICES)))[None, :]
    )
    cols_back = unit(-np.outer(col, col) / COLS)
    rows_back = unit(-(np.outer(row, row) / ROWS + row[:, None] / (4 * ROWS)))
    offset = col[None, :] - col[:, None]
    inside = np.where(offset >= 0, DECAY ** np.maximum(offset, 0), 0.0)
    ends = np.outer(DECAY ** (COLS - 1 - col), DECAY ** (col + 1))
    gap = row[:, None] - row[None, :] - 1
    across = np.where(gap >= 0, DECAY ** (COLS * np.maximum(gap, 0)), 0.0)
    phase = unit((np.arange(ROWS)[:, None] + ROWS * col[None, :] + 0.25) / BLOCK)
    ends_at = DECAY**BLOCK
    reach = (ends_at / DECAY + 1j / DECAY) / (1.0 - 1.0 / (DECAY * phase))
    reach = reach.reshape(2, DEVICES, COLS).transpose(1, 0, 2)
    reach = np.concatenate([reach.real, reach.imag], axis=1)
    reach = np.concatenate([reach, np.zeros_like(reach)], axis=1).astype(np.float32)
    every = np.arange(2 * DEVICES, dtype=np.float64)
    back_all = (
        scaling
        * unit(-np.outer(every, points) / (2 * DEVICES))
        * (1.0 - 1j * unit(points / (2 * DEVICES)))[None, :]
    )
    owner = (blocks.reshape(TEAMS, LANES).T).reshape(-1)
    gap = 2 * owner[:, None] - 1 - every[None, :]
    carry = np.where(gap >= 0, ends_at ** np.maximum(gap, 0), 0.0) @ back_all
    forward = (
        *split(np.concatenate([rows_forward.real, rows_forward.imag])),
        twist.real.astype(np.float32),
        twist.imag.astype(np.float32),
        *split(as_real(cols_forward).T),
    )
    middle = (
        *split(as_real(over_blocks)),
        *split(by_half(as_real(back_blocks))),
        *split(np.concatenate([carry.real, -carry.imag], axis=1)),
    )
    backward = (
        *split(as_real(cols_back).T),
        *split(np.concatenate([rows_back.real, -rows_back.imag], axis=1)),
        *split(np.concatenate([inside, ends], axis=1)),
        *split(across),
    )
    return (*forward, *middle, *backward, reach)


def halves(values):
    high = values.astype(jnp.bfloat16)
    low = (values - high.astype(jnp.float32)).astype(jnp.bfloat16)
    return high, low


def dot(left, right):
    return jnp.dot(left, right, preferred_element_type=jnp.float32)


def times_table(values, table):
    high, low = halves(values)
    return dot(high, table[0][...]) + dot(high, table[1][...]) + dot(low, table[0][...])


def table_times_halves(table, values):
    high, low = values
    return dot(table[0], high) + dot(table[1], high) + dot(table[0], low)


def table_times(table, values):
    return table_times_halves((table[0][...], table[1][...]), halves(values))


def complex_times(left, right):
    return (left[0] * right[0] - left[1] * right[1], left[0] * right[1] + left[1] * right[0])


def row_of(number, place, s, c):
    if number < 2:
        return 8 * s + 4 * number + 2 * place + c
    return 16 + 8 * s + 4 * (number - 2) + 2 * place + c


def block_of(ref, start):
    return ref[pl.ds(start, DEVICES, stride=STEP_IN), :]


def merge_kernel(*refs):
    limbs_in = refs[:OPERANDS]
    count = len(tables())
    tables_in = refs[OPERANDS : OPERANDS + count - 1]
    reach_in = refs[OPERANDS + count - 1]
    sums_out, carry_out = refs[OPERANDS + count : OPERANDS + count + 2]
    rest = refs[OPERANDS + count + 2 :]
    limbs = rest[:OPERANDS]
    held = rest[OPERANDS : OPERANDS + count - 1]
    (
        reach,
        sent,
        landed,
        sent_back,
        landed_back,
        owed,
        owed_in,
        part,
        part_in,
        load_sem,
        table_sem,
        send_sem,
        recv_sem,
        back_send_sem,
        back_recv_sem,
        owed_send_sem,
        owed_recv_sem,
        part_send_sem,
        part_recv_sem,
        relay_sem,
    ) = rest[OPERANDS + count - 1 :]
    (
        rows_high,
        rows_low,
        twist_real,
        twist_imag,
        cols_high,
        cols_low,
        over_high,
        over_low,
        back_high,
        back_low,
        carry_high,
        carry_low,
        cols_back_high,
        cols_back_low,
        rows_back_high,
        rows_back_low,
        scan_high,
        scan_low,
        across_high,
        across_low,
    ) = held
    team, lane = lax.axis_index("grp"), lax.axis_index("lane")
    me = team * LANES + lane

    limb_copies = [
        pltpu.make_async_copy(limbs_in[k], limbs[k], load_sem.at[k]) for k in range(OPERANDS)
    ]
    table_copies = [
        pltpu.make_async_copy(tables_in[k], held[k], table_sem.at[k]) for k in range(count - 1)
    ]
    table_copies.append(
        pltpu.make_async_copy(reach_in.at[me], reach, table_sem.at[count - 1])
    )
    loaded = set()

    def need(*numbers):
        for k in numbers:
            if k not in loaded:
                loaded.add(k)
                table_copies[k].wait()

    first_limbs = [k for group in GROUPS for k in group]
    for k in first_limbs[:2]:
        limb_copies[k].start()
    for k in range(6):
        table_copies[k].start()

    def partner(i):
        other = jnp.bitwise_xor(me, lax.rem(i * 37, DEVICES))
        return other, (lax.div(other, LANES), lax.rem(other, LANES))

    barrier = pltpu.get_barrier_semaphore()

    def greet_lane(i, _):
        other = jnp.bitwise_xor(lane, i)
        pl.semaphore_signal(barrier, inc=1, device_id=(team, other), device_id_type=MESH)
        return 0

    def greet_team(i, _):
        other = jnp.bitwise_xor(team, i)
        pl.semaphore_signal(barrier, inc=1, device_id=(other, lane), device_id_type=MESH)
        return 0

    def relay(i, _):
        other = jnp.bitwise_xor(team, i)
        pl.semaphore_signal(relay_sem, inc=1, device_id=(other, lane), device_id_type=MESH)
        return 0

    lax.fori_loop(1, LANES, greet_lane, 0)
    lax.fori_loop(1, TEAMS, greet_team, 0)
    for k in first_limbs[2:]:
        limb_copies[k].start()
    for k in range(6, count):
        table_copies[k].start()

    def send(source, target, step, offset, size, send_to, recv_at):
        def go(i, _):
            other, place = partner(i)
            pltpu.make_async_remote_copy(
                src_ref=source.at[pl.ds(pl.multiple_of(other * step, 8) + offset, size)],
                dst_ref=target.at[pl.ds(pl.multiple_of(me * step, 8) + offset, size)],
                send_sem=send_to,
                recv_sem=recv_at,
                device_id=place,
                device_id_type=MESH,
            ).start()
            return 0

        lax.fori_loop(1, DEVICES, go, 0)
        here = pl.ds(pl.multiple_of(me * step, 8) + offset, size)
        target[here, :] = source[here, :]

    def wait(ref, size, sem, senders=DEVICES):
        whole = ref.at[pl.ds(0, (senders - 1) * size)]
        pltpu.make_async_copy(whole, whole, sem).wait()

    def transform(number):
        for k in GROUPS[number]:
            limb_copies[k].wait()
        whole = jnp.concatenate([limbs[k][...] for k in GROUPS[number]], axis=1)
        whole = whole.astype(jnp.bfloat16)
        first = dot(rows_high[...], whole) + dot(rows_low[...], whole)
        for place in range(len(GROUPS[number])):
            cols = slice(place * COLS, (place + 1) * COLS)
            turned = complex_times(
                (first[:ROWS, cols], first[ROWS:, cols]), (twist_real[...], twist_imag[...])
            )
            done = times_table(jnp.concatenate(turned, axis=1), (cols_high, cols_low))
            for s in range(2):
                for c in range(2):
                    start = row_of(number, place, s, c)
                    sent[pl.ds(start, DEVICES, stride=STEP_IN), :] = done[
                        s * DEVICES : (s + 1) * DEVICES, c * COLS : (c + 1) * COLS
                    ]

    def send_group(number):
        send(
            sent, landed, STEP_IN, 8 * number, SIZES[number],
            send_sem.at[number], recv_sem.at[number],
        )

    by_s = [[] for _ in range(OPERANDS)]
    bessel, harmonic = [], []

    def tile(number):
        return pl.ds(pl.multiple_of(number * 8, 8), 8)

    def arrive_rest(s):
        wait(landed, SIZES[2 + s], recv_sem.at[2 + s])
        slots = [(number, place) for number in (2, 3) for place in range(len(GROUPS[number]))]
        parts = [
            jnp.concatenate(
                [block_of(landed, row_of(number, place, s, c)) for number, place in slots], axis=1
            )
            for c in range(2)
        ]
        both = table_times((over_high, over_low), jnp.concatenate(parts, axis=0))
        for slot, (number, place) in enumerate(slots):
            cols = slice(slot * COLS, (slot + 1) * COLS)
            by_s[GROUPS[number][place]].append(
                (both[: 2 * DEVICES, cols], both[2 * DEVICES :, cols])
            )
        terms = [complex_times(by_s[a][s], by_s[b][s]) for a, b in ((4, 1), (0, 5), (6, 3))]
        harmonic.append((sum(t[0] for t in terms), sum(t[1] for t in terms)))

    def invert_half(number, s):
        piece = (bessel, harmonic)[number][s]
        product = halves(jnp.concatenate(piece, axis=0))
        back = table_times_halves((back_high[...], back_low[...]), product)
        for part in range(4):
            sent_back[number, s, pl.ds(part, DEVICES, stride=STEP_OUT), :] = back[
                part * DEVICES : (part + 1) * DEVICES
            ]

    def send_back(number, s):
        send(
            sent_back.at[number, s], landed_back.at[number, s], STEP_OUT, 0, 4,
            back_send_sem.at[number, s], back_recv_sem.at[number, s],
        )

    def settle(number):
        pieces = (bessel, harmonic)[number]
        product = tuple(
            jnp.concatenate([piece[c] for piece in pieces], axis=1) for c in range(2)
        )
        reached = [
            complex_times(
                (product[0][:, s * COLS : (s + 1) * COLS], product[1][:, s * COLS : (s + 1) * COLS]),
                (reach[s : s + 1, :], reach[2 + s : 3 + s, :]),
            )
            for s in range(2)
        ]
        reached = jnp.concatenate(
            [reached[0][0] + reached[1][0], reached[0][1] + reached[1][1]], axis=0
        )
        owed[number] = table_times((carry_high, carry_low), reached)

        def owe(i, _):
            other = jnp.bitwise_xor(lane, i)
            pltpu.make_async_remote_copy(
                src_ref=owed.at[number, tile(other)],
                dst_ref=owed_in.at[number, tile(lane)],
                send_sem=owed_send_sem.at[number],
                recv_sem=owed_recv_sem.at[number],
                device_id=(team, other),
                device_id_type=MESH,
            ).start()
            return 0

        lax.fori_loop(1, LANES, owe, 0)
        owed_in[number, tile(lane), :] = owed[number, tile(lane), :]

    def arrive_half(s):
        wait(landed, SIZES[s], recv_sem.at[s])
        for number in range(2):
            parts = [
                jnp.concatenate(
                    [block_of(landed, row_of(number, place, s, c)) for place in range(2)], axis=1
                )
                for c in range(2)
            ]
            both = table_times((over_high, over_low), jnp.concatenate(parts, axis=0))
            for place, k in enumerate(GROUPS[number]):
                cols = slice(place * COLS, (place + 1) * COLS)
                by_s[k].append((both[: 2 * DEVICES, cols], both[2 * DEVICES :, cols]))
        terms = [complex_times(by_s[a][s], by_s[b][s]) for a, b in ((2, 1), (0, 3))]
        bessel.append((terms[0][0] + terms[1][0], terms[0][1] + terms[1][1]))

    def gather_owed(number):
        wait(owed_in.at[number], 8, owed_recv_sem.at[number], LANES)
        part[number] = sum(owed_in[number, 8 * k : 8 * k + 8, :] for k in range(LANES))

        def pay(i, _):
            pltpu.make_async_remote_copy(
                src_ref=part.at[number],
                dst_ref=part_in.at[number, tile(team)],
                send_sem=part_send_sem.at[number],
                recv_sem=part_recv_sem.at[number],
                device_id=(jnp.bitwise_xor(team, i), lane),
                device_id_type=MESH,
            ).start()
            return 0

        lax.fori_loop(1, TEAMS, pay, 0)
        part_in[number, tile(team), :] = part[number]

    def finish(number, odd):
        if not odd:
            for s in range(2):
                wait(landed_back.at[number, s], 4, back_recv_sem.at[number, s])

        def piece(s, c):
            row = pl.ds(2 * odd + c, DEVICES, stride=STEP_OUT)
            return landed_back[number, s, row, :]

        spectrum = jnp.concatenate(
            [jnp.concatenate([piece(s, c) for c in range(2)], axis=1) for s in range(2)], axis=0
        )
        first = times_table(spectrum, (cols_back_high, cols_back_low))
        turned = complex_times(
            (first[:, :COLS], first[:, COLS:]), (twist_real[...], -twist_imag[...])
        )
        coeffs = table_times((rows_back_high, rows_back_low), jnp.concatenate(turned, axis=0))
        both = times_table(coeffs, (scan_high, scan_low))
        sums_out[number, odd * ROWS : (odd + 1) * ROWS, :] = both[:, :COLS] + table_times(
            (across_high, across_low), both[:, COLS:]
        )

    need(0, 1, 2, 3, 4, 5)
    transform(0)
    pl.semaphore_wait(barrier, LANES + TEAMS - 2)
    lax.fori_loop(1, TEAMS, relay, 0)
    transform(1)
    pl.semaphore_wait(relay_sem, TEAMS - 1)
    send_group(0)
    send_group(1)
    transform(2)
    transform(3)
    send_group(2)
    send_group(3)
    need(6, 7)
    arrive_half(0)
    need(8, 9, 10, 11, count - 1)
    invert_half(0, 0)
    send_back(0, 0)
    arrive_half(1)
    invert_half(0, 1)
    send_back(0, 1)
    arrive_rest(0)
    invert_half(1, 0)
    send_back(1, 0)
    arrive_rest(1)
    settle(0)
    settle(1)
    invert_half(1, 1)
    send_back(1, 1)
    gather_owed(0)
    need(*range(count))
    finish(0, 0)
    gather_owed(1)
    finish(0, 1)
    finish(1, 0)
    finish(1, 1)

    mine = lax.broadcasted_iota(jnp.int32, (8, COLS), 0) == team
    for number in range(OUTPUTS):
        wait(part_in.at[number], 8, part_recv_sem.at[number], TEAMS)
        total = sum(part_in[number, 8 * k : 8 * k + 8, :] for k in range(TEAMS))
        carry_out[number] = jnp.where(mine, total, 0.0)
    for number, size in enumerate(SIZES):
        wait(sent, size, send_sem.at[number])
    for number in range(OUTPUTS):
        for odd in range(2):
            wait(sent_back.at[number, odd], 4, back_send_sem.at[number, odd])
        wait(owed.at[number], 8, owed_send_sem.at[number], LANES)
        wait(part_in.at[number], 8, part_send_sem.at[number], TEAMS)


def carry_kernel(sums, carry, *refs):
    outs = refs[:OUTPUTS]
    results, out_sem = refs[OUTPUTS:]
    shape = (ROWS, COLS)
    place = lax.broadcasted_iota(jnp.int32, shape, 0) * COLS + lax.broadcasted_iota(
        jnp.int32, shape, 1
    )
    power = jnp.exp((place + 1).astype(jnp.float32) * (-1.0 / (2 * BLOCK)))
    corner = place[:8, :] == 8 * COLS - 1
    copies = []
    for k in range(OUTPUTS):
        incoming = jnp.sum(carry[k])
        for odd in range(2):
            rows = pl.ds(odd * ROWS, ROWS)
            results[k, rows, :] = sums[k, rows, :] + incoming * power
            copy = pltpu.make_async_copy(
                results.at[k, rows], outs[k].at[rows], out_sem.at[k, odd]
            )
            copy.start()
            copies.append(copy)
            last = sums[k, (odd + 1) * ROWS - 8 : (odd + 1) * ROWS, :]
            incoming = incoming * DECAY**BLOCK + jnp.sum(jnp.where(corner, last, 0.0))
    for copy in copies:
        copy.wait()


def local(*operands):
    limbs = [v.reshape(ROWS, COLS) for v in operands]
    constants = tables()
    anywhere = pl.BlockSpec(memory_space=pl.ANY)
    on_chip = pl.BlockSpec(memory_space=pltpu.VMEM)
    sums_shape = (OUTPUTS, 2 * ROWS, COLS)
    sums, carry = pl.pallas_call(
        merge_kernel,
        out_shape=[
            jax.ShapeDtypeStruct(sums_shape, jnp.float32),
            jax.ShapeDtypeStruct((OUTPUTS, 8, COLS), jnp.float32),
        ],
        in_specs=[anywhere] * (OPERANDS + len(constants)),
        out_specs=[on_chip] * 2,
        scratch_shapes=[
            *[pltpu.VMEM((ROWS, COLS), jnp.float32)] * OPERANDS,
            *[pltpu.VMEM(t.shape, t.dtype) for t in constants[:-1]],
            pltpu.VMEM(constants[-1].shape[1:], jnp.float32),
            pltpu.VMEM((DEVICES * STEP_IN, COLS), jnp.float32),
            pltpu.VMEM((DEVICES * STEP_IN, COLS), jnp.float32),
            *[pltpu.VMEM((OUTPUTS, 2, DEVICES * STEP_OUT, COLS), jnp.float32)] * 2,
            pltpu.VMEM((OUTPUTS, DEVICES, COLS), jnp.float32),
            pltpu.VMEM((OUTPUTS, DEVICES, COLS), jnp.float32),
            pltpu.VMEM((OUTPUTS, 8, COLS), jnp.float32),
            pltpu.VMEM((OUTPUTS, 8 * TEAMS, COLS), jnp.float32),
            pltpu.SemaphoreType.DMA((OPERANDS,)),
            pltpu.SemaphoreType.DMA((len(constants),)),
            *[pltpu.SemaphoreType.DMA((len(GROUPS),))] * 2,
            *[pltpu.SemaphoreType.DMA((OUTPUTS, 2))] * 2,
            *[pltpu.SemaphoreType.DMA((OUTPUTS,))] * 4,
            pltpu.SemaphoreType.REGULAR,
        ],
        compiler_params=pltpu.CompilerParams(
            collective_id=0, has_side_effects=True, vmem_limit_bytes=40 << 20
        ),
    )(*[pltpu.with_memory_space_constraint(v, pltpu.HBM) for v in (*limbs, *constants)])
    results = pl.pallas_call(
        carry_kernel,
        out_shape=[jax.ShapeDtypeStruct(sums_shape[1:], jnp.float32)] * OUTPUTS,
        in_specs=[on_chip] * 2,
        out_specs=[anywhere] * OUTPUTS,
        scratch_shapes=[
            pltpu.VMEM(sums_shape, jnp.float32),
            pltpu.SemaphoreType.DMA((OUTPUTS, 2)),
        ],
        compiler_params=pltpu.CompilerParams(vmem_limit_bytes=8 << 20),
    )(sums, carry)
    return tuple(r.reshape(-1) for r in results)


def solution(mesh):
    return jax.shard_map(
        local,
        mesh=mesh,
        in_specs=(P(AXES),) * OPERANDS,
        out_specs=(P(AXES),) * OUTPUTS,
        check_vma=False,
    )
```

```python
import functools
import math

import jax
import jax.numpy as jnp
import numpy as np
from jax import lax
from jax.experimental import pallas as pl
from jax.experimental.pallas import tpu as pltpu
from jax.sharding import PartitionSpec as P

AXES = ("grp", "lane")
DEVICES = 128
BLOCK = 32768
ROWS = 256
COLS = 128
OPERANDS = 7
OUTPUTS = 2
DECAY = math.exp(-1.0 / (2 * BLOCK))
LANES = 16
TEAMS = 8
STEP_IN = 32
STEP_OUT = 8
GROUPS = ((0, 3), (2, 1), (4, 5), (6,))
SIZES = (8, 8, 6, 6)
MESH = pl.DeviceIdType.MESH


def split(table):
    high = table.astype(jnp.bfloat16)
    low = (table - high.astype(np.float64)).astype(jnp.bfloat16)
    return high, low


def as_real(table):
    return np.block([[table.real, -table.imag], [table.imag, table.real]])


def by_half(table):
    parts = table.reshape(2, 2, DEVICES, -1).transpose(1, 0, 2, 3)
    return parts.reshape(4 * DEVICES, -1)


def unit(turns):
    return np.exp(2j * math.pi * (turns % 1.0))


@functools.lru_cache(maxsize=None)
def tables():
    row = np.arange(ROWS, dtype=np.float64)
    col = np.arange(COLS, dtype=np.float64)
    rows_forward = unit(np.outer(row, row) / ROWS + row[None, :] / (4 * ROWS))
    twist = unit(np.outer(row + 0.25, col) / BLOCK)
    cols_forward = unit(np.outer(col, col) / COLS)
    blocks = np.arange(DEVICES, dtype=np.float64)
    points = np.arange(2 * DEVICES, dtype=np.float64)
    over_blocks = unit(np.outer(points, blocks) / (2 * DEVICES))
    total = DEVICES * BLOCK
    scaling = 1.0 / (16.0 * math.sqrt(total) * math.sqrt(BLOCK)) / (2 * DEVICES) / BLOCK
    order = np.concatenate([2 * blocks, 2 * blocks + 1])
    back_blocks = (
        scaling
        * unit(-np.outer(order, points) / (2 * DEVICES))
        * (1.0 - 1j * unit(points / (2 * DEVICES)))[None, :]
    )
    cols_back = unit(-np.outer(col, col) / COLS)
    rows_back = unit(-(np.outer(row, row) / ROWS + row[:, None] / (4 * ROWS)))
    offset = col[None, :] - col[:, None]
    inside = np.where(offset >= 0, DECAY ** np.maximum(offset, 0), 0.0)
    ends = np.outer(DECAY ** (COLS - 1 - col), DECAY ** (col + 1))
    gap = row[:, None] - row[None, :] - 1
    across = np.where(gap >= 0, DECAY ** (COLS * np.maximum(gap, 0)), 0.0)
    phase = unit((np.arange(ROWS)[:, None] + ROWS * col[None, :] + 0.25) / BLOCK)
    ends_at = DECAY**BLOCK
    reach = (ends_at / DECAY + 1j / DECAY) / (1.0 - 1.0 / (DECAY * phase))
    reach = reach.reshape(2, DEVICES, COLS).transpose(1, 0, 2)
    reach = np.concatenate([reach.real, reach.imag], axis=1)
    reach = np.concatenate([reach, np.zeros_like(reach)], axis=1).astype(np.float32)
    every = np.arange(2 * DEVICES, dtype=np.float64)
    back_all = (
        scaling
        * unit(-np.outer(every, points) / (2 * DEVICES))
        * (1.0 - 1j * unit(points / (2 * DEVICES)))[None, :]
    )
    owner = (blocks.reshape(TEAMS, LANES).T).reshape(-1)
    gap = 2 * owner[:, None] - 1 - every[None, :]
    carry = np.where(gap >= 0, ends_at ** np.maximum(gap, 0), 0.0) @ back_all
    forward = (
        *split(np.concatenate([rows_forward.real, rows_forward.imag])),
        twist.real.astype(np.float32),
        twist.imag.astype(np.float32),
        *split(as_real(cols_forward).T),
    )
    middle = (
        *split(as_real(over_blocks)),
        *split(by_half(as_real(back_blocks))),
        *split(np.concatenate([carry.real, -carry.imag], axis=1)),
    )
    backward = (
        *split(as_real(cols_back).T),
        *split(np.concatenate([rows_back.real, -rows_back.imag], axis=1)),
        *split(np.concatenate([inside, ends], axis=1)),
        *split(across),
    )
    return (*forward, *middle, *backward, reach)


def halves(values):
    high = values.astype(jnp.bfloat16)
    low = (values - high.astype(jnp.float32)).astype(jnp.bfloat16)
    return high, low


def dot(left, right):
    return jnp.dot(left, right, preferred_element_type=jnp.float32)


def times_table(values, table):
    high, low = halves(values)
    return dot(high, table[0][...]) + dot(high, table[1][...]) + dot(low, table[0][...])


def table_times_halves(table, values):
    high, low = values
    return dot(table[0], high) + dot(table[1], high) + dot(table[0], low)


def table_times(table, values):
    return table_times_halves((table[0][...], table[1][...]), halves(values))


def complex_times(left, right):
    return (left[0] * right[0] - left[1] * right[1], left[0] * right[1] + left[1] * right[0])


def row_of(number, place, s, c):
    if number < 2:
        return 8 * s + 4 * number + 2 * place + c
    return 16 + 8 * s + 4 * (number - 2) + 2 * place + c


def block_of(ref, start):
    return ref[pl.ds(start, DEVICES, stride=STEP_IN), :]


def merge_kernel(*refs):
    limbs_in = refs[:OPERANDS]
    count = len(tables())
    tables_in = refs[OPERANDS : OPERANDS + count - 1]
    reach_in = refs[OPERANDS + count - 1]
    sums_out, carry_out = refs[OPERANDS + count : OPERANDS + count + 2]
    rest = refs[OPERANDS + count + 2 :]
    limbs = rest[:OPERANDS]
    held = rest[OPERANDS : OPERANDS + count - 1]
    (
        reach,
        sent,
        landed,
        sent_back,
        landed_back,
        owed,
        owed_in,
        part,
        part_in,
        load_sem,
        table_sem,
        send_sem,
        recv_sem,
        back_send_sem,
        back_recv_sem,
        owed_send_sem,
        owed_recv_sem,
        part_send_sem,
        part_recv_sem,
        relay_sem,
    ) = rest[OPERANDS + count - 1 :]
    (
        rows_high,
        rows_low,
        twist_real,
        twist_imag,
        cols_high,
        cols_low,
        over_high,
        over_low,
        back_high,
        back_low,
        carry_high,
        carry_low,
        cols_back_high,
        cols_back_low,
        rows_back_high,
        rows_back_low,
        scan_high,
        scan_low,
        across_high,
        across_low,
    ) = held
    team, lane = lax.axis_index("grp"), lax.axis_index("lane")
    me = team * LANES + lane

    limb_copies = [
        pltpu.make_async_copy(limbs_in[k], limbs[k], load_sem.at[k]) for k in range(OPERANDS)
    ]
    table_copies = [
        pltpu.make_async_copy(tables_in[k], held[k], table_sem.at[k]) for k in range(count - 1)
    ]
    table_copies.append(
        pltpu.make_async_copy(reach_in.at[me], reach, table_sem.at[count - 1])
    )
    loaded = set()

    def need(*numbers):
        for k in numbers:
            if k not in loaded:
                loaded.add(k)
                table_copies[k].wait()

    first_limbs = [k for group in GROUPS for k in group]
    for k in first_limbs[:2]:
        limb_copies[k].start()
    for k in range(6):
        table_copies[k].start()

    def partner(i):
        other = jnp.bitwise_xor(me, lax.rem(i * 37, DEVICES))
        return other, (lax.div(other, LANES), lax.rem(other, LANES))

    barrier = pltpu.get_barrier_semaphore()

    def greet_lane(i, _):
        other = jnp.bitwise_xor(lane, i)
        pl.semaphore_signal(barrier, inc=1, device_id=(team, other), device_id_type=MESH)
        return 0

    def greet_team(i, _):
        other = jnp.bitwise_xor(team, i)
        pl.semaphore_signal(barrier, inc=1, device_id=(other, lane), device_id_type=MESH)
        return 0

    def relay(i, _):
        other = jnp.bitwise_xor(team, i)
        pl.semaphore_signal(relay_sem, inc=1, device_id=(other, lane), device_id_type=MESH)
        return 0

    lax.fori_loop(1, LANES, greet_lane, 0)
    lax.fori_loop(1, TEAMS, greet_team, 0)
    for k in first_limbs[2:]:
        limb_copies[k].start()
    for k in range(6, count):
        table_copies[k].start()

    def send(source, target, step, offset, size, send_to, recv_at):
        def go(i, _):
            other, place = partner(i)
            pltpu.make_async_remote_copy(
                src_ref=source.at[pl.ds(pl.multiple_of(other * step, 8) + offset, size)],
                dst_ref=target.at[pl.ds(pl.multiple_of(me * step, 8) + offset, size)],
                send_sem=send_to,
                recv_sem=recv_at,
                device_id=place,
                device_id_type=MESH,
            ).start()
            return 0

        lax.fori_loop(1, DEVICES, go, 0)
        here = pl.ds(pl.multiple_of(me * step, 8) + offset, size)
        target[here, :] = source[here, :]

    def wait(ref, size, sem, senders=DEVICES):
        whole = ref.at[pl.ds(0, (senders - 1) * size)]
        pltpu.make_async_copy(whole, whole, sem).wait()

    def transform(number):
        for k in GROUPS[number]:
            limb_copies[k].wait()
        whole = jnp.concatenate([limbs[k][...] for k in GROUPS[number]], axis=1)
        whole = whole.astype(jnp.bfloat16)
        first = dot(rows_high[...], whole) + dot(rows_low[...], whole)
        for place in range(len(GROUPS[number])):
            cols = slice(place * COLS, (place + 1) * COLS)
            turned = complex_times(
                (first[:ROWS, cols], first[ROWS:, cols]), (twist_real[...], twist_imag[...])
            )
            done = times_table(jnp.concatenate(turned, axis=1), (cols_high, cols_low))
            for s in range(2):
                for c in range(2):
                    start = row_of(number, place, s, c)
                    sent[pl.ds(start, DEVICES, stride=STEP_IN), :] = done[
                        s * DEVICES : (s + 1) * DEVICES, c * COLS : (c + 1) * COLS
                    ]

    def send_group(number):
        send(
            sent, landed, STEP_IN, 8 * number, SIZES[number],
            send_sem.at[number], recv_sem.at[number],
        )

    by_s = [[] for _ in range(OPERANDS)]
    bessel, harmonic = [], []

    def tile(number):
        return pl.ds(pl.multiple_of(number * 8, 8), 8)

    def arrive_rest(s):
        wait(landed, SIZES[2 + s], recv_sem.at[2 + s])
        slots = [(number, place) for number in (2, 3) for place in range(len(GROUPS[number]))]
        parts = [
            jnp.concatenate(
                [block_of(landed, row_of(number, place, s, c)) for number, place in slots], axis=1
            )
            for c in range(2)
        ]
        both = table_times((over_high, over_low), jnp.concatenate(parts, axis=0))
        for slot, (number, place) in enumerate(slots):
            cols = slice(slot * COLS, (slot + 1) * COLS)
            by_s[GROUPS[number][place]].append(
                (both[: 2 * DEVICES, cols], both[2 * DEVICES :, cols])
            )
        terms = [complex_times(by_s[a][s], by_s[b][s]) for a, b in ((4, 1), (0, 5), (6, 3))]
        harmonic.append((sum(t[0] for t in terms), sum(t[1] for t in terms)))

    def invert_half(number, s):
        piece = (bessel, harmonic)[number][s]
        product = halves(jnp.concatenate(piece, axis=0))
        back = table_times_halves((back_high[...], back_low[...]), product)
        for part in range(4):
            sent_back[number, s, pl.ds(part, DEVICES, stride=STEP_OUT), :] = back[
                part * DEVICES : (part + 1) * DEVICES
            ]

    def send_back(number, s):
        send(
            sent_back.at[number, s], landed_back.at[number, s], STEP_OUT, 0, 4,
            back_send_sem.at[number, s], back_recv_sem.at[number, s],
        )

    def settle(number):
        pieces = (bessel, harmonic)[number]
        product = tuple(
            jnp.concatenate([piece[c] for piece in pieces], axis=1) for c in range(2)
        )
        reached = [
            complex_times(
                (product[0][:, s * COLS : (s + 1) * COLS], product[1][:, s * COLS : (s + 1) * COLS]),
                (reach[s : s + 1, :], reach[2 + s : 3 + s, :]),
            )
            for s in range(2)
        ]
        reached = jnp.concatenate(
            [reached[0][0] + reached[1][0], reached[0][1] + reached[1][1]], axis=0
        )
        owed[number] = table_times((carry_high, carry_low), reached)

        def owe(i, _):
            other = jnp.bitwise_xor(lane, i)
            pltpu.make_async_remote_copy(
                src_ref=owed.at[number, tile(other)],
                dst_ref=owed_in.at[number, tile(lane)],
                send_sem=owed_send_sem.at[number],
                recv_sem=owed_recv_sem.at[number],
                device_id=(team, other),
                device_id_type=MESH,
            ).start()
            return 0

        lax.fori_loop(1, LANES, owe, 0)
        owed_in[number, tile(lane), :] = owed[number, tile(lane), :]

    def arrive_half(s):
        wait(landed, SIZES[s], recv_sem.at[s])
        for number in range(2):
            parts = [
                jnp.concatenate(
                    [block_of(landed, row_of(number, place, s, c)) for place in range(2)], axis=1
                )
                for c in range(2)
            ]
            both = table_times((over_high, over_low), jnp.concatenate(parts, axis=0))
            for place, k in enumerate(GROUPS[number]):
                cols = slice(place * COLS, (place + 1) * COLS)
                by_s[k].append((both[: 2 * DEVICES, cols], both[2 * DEVICES :, cols]))
        terms = [complex_times(by_s[a][s], by_s[b][s]) for a, b in ((2, 1), (0, 3))]
        bessel.append((terms[0][0] + terms[1][0], terms[0][1] + terms[1][1]))

    def gather_owed(number):
        wait(owed_in.at[number], 8, owed_recv_sem.at[number], LANES)
        part[number] = sum(owed_in[number, 8 * k : 8 * k + 8, :] for k in range(LANES))

        def pay(i, _):
            pltpu.make_async_remote_copy(
                src_ref=part.at[number],
                dst_ref=part_in.at[number, tile(team)],
                send_sem=part_send_sem.at[number],
                recv_sem=part_recv_sem.at[number],
                device_id=(jnp.bitwise_xor(team, i), lane),
                device_id_type=MESH,
            ).start()
            return 0

        lax.fori_loop(1, TEAMS, pay, 0)
        part_in[number, tile(team), :] = part[number]

    def finish(number, odd):
        if not odd:
            for s in range(2):
                wait(landed_back.at[number, s], 4, back_recv_sem.at[number, s])

        def piece(s, c):
            row = pl.ds(2 * odd + c, DEVICES, stride=STEP_OUT)
            return landed_back[number, s, row, :]

        spectrum = jnp.concatenate(
            [jnp.concatenate([piece(s, c) for c in range(2)], axis=1) for s in range(2)], axis=0
        )
        first = times_table(spectrum, (cols_back_high, cols_back_low))
        turned = complex_times(
            (first[:, :COLS], first[:, COLS:]), (twist_real[...], -twist_imag[...])
        )
        coeffs = table_times((rows_back_high, rows_back_low), jnp.concatenate(turned, axis=0))
        both = times_table(coeffs, (scan_high, scan_low))
        sums_out[number, odd * ROWS : (odd + 1) * ROWS, :] = both[:, :COLS] + table_times(
            (across_high, across_low), both[:, COLS:]
        )

    need(0, 1, 2, 3, 4, 5)
    transform(0)
    pl.semaphore_wait(barrier, LANES + TEAMS - 2)
    lax.fori_loop(1, TEAMS, relay, 0)
    transform(1)
    pl.semaphore_wait(relay_sem, TEAMS - 1)
    send_group(0)
    send_group(1)
    transform(2)
    transform(3)
    send_group(2)
    send_group(3)
    need(6, 7)
    arrive_half(0)
    need(8, 9, 10, 11, count - 1)
    invert_half(0, 0)
    send_back(0, 0)
    arrive_half(1)
    invert_half(0, 1)
    send_back(0, 1)
    arrive_rest(0)
    invert_half(1, 0)
    send_back(1, 0)
    settle(0)
    arrive_rest(1)
    settle(1)
    invert_half(1, 1)
    send_back(1, 1)
    gather_owed(0)
    need(*range(count))
    finish(0, 0)
    gather_owed(1)
    finish(0, 1)
    finish(1, 0)
    finish(1, 1)

    mine = lax.broadcasted_iota(jnp.int32, (8, COLS), 0) == team
    for number in range(OUTPUTS):
        wait(part_in.at[number], 8, part_recv_sem.at[number], TEAMS)
        total = sum(part_in[number, 8 * k : 8 * k + 8, :] for k in range(TEAMS))
        carry_out[number] = jnp.where(mine, total, 0.0)
    for number, size in enumerate(SIZES):
        wait(sent, size, send_sem.at[number])
    for number in range(OUTPUTS):
        for odd in range(2):
            wait(sent_back.at[number, odd], 4, back_send_sem.at[number, odd])
        wait(owed.at[number], 8, owed_send_sem.at[number], LANES)
        wait(part_in.at[number], 8, part_send_sem.at[number], TEAMS)


def carry_kernel(sums, carry, *refs):
    outs = refs[:OUTPUTS]
    results, out_sem = refs[OUTPUTS:]
    shape = (ROWS, COLS)
    place = lax.broadcasted_iota(jnp.int32, shape, 0) * COLS + lax.broadcasted_iota(
        jnp.int32, shape, 1
    )
    power = jnp.exp((place + 1).astype(jnp.float32) * (-1.0 / (2 * BLOCK)))
    corner = place[:8, :] == 8 * COLS - 1
    copies = []
    for k in range(OUTPUTS):
        incoming = jnp.sum(carry[k])
        for odd in range(2):
            rows = pl.ds(odd * ROWS, ROWS)
            results[k, rows, :] = sums[k, rows, :] + incoming * power
            copy = pltpu.make_async_copy(
                results.at[k, rows], outs[k].at[rows], out_sem.at[k, odd]
            )
            copy.start()
            copies.append(copy)
            last = sums[k, (odd + 1) * ROWS - 8 : (odd + 1) * ROWS, :]
            incoming = incoming * DECAY**BLOCK + jnp.sum(jnp.where(corner, last, 0.0))
    for copy in copies:
        copy.wait()


def local(*operands):
    limbs = [v.reshape(ROWS, COLS) for v in operands]
    constants = tables()
    anywhere = pl.BlockSpec(memory_space=pl.ANY)
    on_chip = pl.BlockSpec(memory_space=pltpu.VMEM)
    sums_shape = (OUTPUTS, 2 * ROWS, COLS)
    sums, carry = pl.pallas_call(
        merge_kernel,
        out_shape=[
            jax.ShapeDtypeStruct(sums_shape, jnp.float32),
            jax.ShapeDtypeStruct((OUTPUTS, 8, COLS), jnp.float32),
        ],
        in_specs=[anywhere] * (OPERANDS + len(constants)),
        out_specs=[on_chip] * 2,
        scratch_shapes=[
            *[pltpu.VMEM((ROWS, COLS), jnp.float32)] * OPERANDS,
            *[pltpu.VMEM(t.shape, t.dtype) for t in constants[:-1]],
            pltpu.VMEM(constants[-1].shape[1:], jnp.float32),
            pltpu.VMEM((DEVICES * STEP_IN, COLS), jnp.float32),
            pltpu.VMEM((DEVICES * STEP_IN, COLS), jnp.float32),
            *[pltpu.VMEM((OUTPUTS, 2, DEVICES * STEP_OUT, COLS), jnp.float32)] * 2,
            pltpu.VMEM((OUTPUTS, DEVICES, COLS), jnp.float32),
            pltpu.VMEM((OUTPUTS, DEVICES, COLS), jnp.float32),
            pltpu.VMEM((OUTPUTS, 8, COLS), jnp.float32),
            pltpu.VMEM((OUTPUTS, 8 * TEAMS, COLS), jnp.float32),
            pltpu.SemaphoreType.DMA((OPERANDS,)),
            pltpu.SemaphoreType.DMA((len(constants),)),
            *[pltpu.SemaphoreType.DMA((len(GROUPS),))] * 2,
            *[pltpu.SemaphoreType.DMA((OUTPUTS, 2))] * 2,
            *[pltpu.SemaphoreType.DMA((OUTPUTS,))] * 4,
            pltpu.SemaphoreType.REGULAR,
        ],
        compiler_params=pltpu.CompilerParams(
            collective_id=0, has_side_effects=True, vmem_limit_bytes=40 << 20
        ),
    )(*[pltpu.with_memory_space_constraint(v, pltpu.HBM) for v in (*limbs, *constants)])
    results = pl.pallas_call(
        carry_kernel,
        out_shape=[jax.ShapeDtypeStruct(sums_shape[1:], jnp.float32)] * OUTPUTS,
        in_specs=[on_chip] * 2,
        out_specs=[anywhere] * OUTPUTS,
        scratch_shapes=[
            pltpu.VMEM(sums_shape, jnp.float32),
            pltpu.SemaphoreType.DMA((OUTPUTS, 2)),
        ],
        compiler_params=pltpu.CompilerParams(vmem_limit_bytes=8 << 20),
    )(sums, carry)
    return tuple(r.reshape(-1) for r in results)


def solution(mesh):
    return jax.shard_map(
        local,
        mesh=mesh,
        in_specs=(P(AXES),) * OPERANDS,
        out_specs=(P(AXES),) * OUTPUTS,
        check_vma=False,
    )
```
